128 devices in a mesh: dp: 16 (over x, y_hi, core), code: 8 (over y_lo, z).
Axes of the slice: x: 4, y: 4 (y_hi: 2, y_lo: 2; y = y_hi * 2 + y_lo), z: 4, core: 2. Of those that a mesh axis runs over, the one named last changes fastest.
Arguments:
- temporal_out: bfloat16 [2048, 4096], P('dp'), may hold values from -6 to 6
- depth_in: bfloat16 [8, 4096, 1024], P('code', 'dp'), may hold values from -0.09375 to 0.09375
- embed: bfloat16 [8, 1024, 1024], P('code'), may hold values from -6 to 6
- depth_w1: bfloat16 [8, 1024, 2112], P('code', None, 'dp'), may hold values from -0.1875 to 0.1875
- depth_w2: bfloat16 [8, 1024, 2112], P('code', None, 'dp'), may hold values from -0.125 to 0.125
- audio_tokens: int32 [2048, 8], P(None, 'code'), may hold values from 0 to 1023
- barge_mask: int32 [2048], P('dp'), may hold values 0 or 1
- out_grad: bfloat16 [2048, 8, 1024], P('dp', 'code'), may hold values from -6 to 6
Outputs:
- temporal_grad: bfloat16 [2048, 4096], P('dp', 'code')
- depth_in_grad: bfloat16 [8, 4096, 1024], P('code', 'dp')
- embed_grad: bfloat16 [8, 1024, 1024], P('code', 'dp')
- w1_grad: bfloat16 [8, 1024, 2112], P('code', None, 'dp')
- w2_grad: bfloat16 [8, 1024, 2112], P('code', None, 'dp')
The draws below stay inside these ranges and needn't reach their ends.
All inputs are finite; a program needn't handle non-finite values. No bound on the sum of `barge_mask` on one device may be relied on, other than what follows from the above.
Results may differ from the reference program's by a relative error of at most 0.02.
Values may be sent and summed in bfloat16 or wider, within the bound.
No kernel may reach another device: no remote copies, remote signals or barrier semaphores. Data moves between devices by JAX's collectives and lax.ppermute only.
A program may use at most 128 MiB of HBM per device.

```python
import jax
import jax.numpy as jnp
from jax import lax

D = 4096
DD = 1024
DH = 2112
V = 1024
ROWS_DEV = 128
FRAMES = 2048
CODEBOOKS = 8
N_DP = 16


def plant(entries, key, least, high):
    place = [jax.random.randint(jax.random.fold_in(key, axis), (), 0, length) for axis, length in enumerate(entries.shape)]
    main_axis = entries.shape.index(max(entries.shape))
    next_to = place[:main_axis] + [(place[main_axis] + 1) % entries.shape[main_axis]] + place[main_axis + 1:]
    return entries.at[tuple(place)].set(least).at[tuple(next_to)].set(high)


def levels(key, shape, cuts, low, top_value):
    def one(position, parts):
        heights = jax.random.uniform(jax.random.fold_in(jax.random.fold_in(key, 6), position), (parts,), jnp.float32, low / len(cuts), top_value / len(cuts))
        return jnp.repeat(jnp.exp(heights), shape[position] // parts).reshape((-1,) + (1,) * (len(shape) - position - 1))

    gain = one(*cuts[0])
    for cut in cuts[1:]:
        gain = gain * one(*cut)
    return gain


def noise(key, extent, deviation, bound, pieces=(), held_as=jnp.bfloat16):
    level = levels(key, extent, pieces, -0.22, 0.18) if pieces else 1.0
    values = jax.random.normal(key, extent, jnp.float32) * deviation * level
    return jnp.minimum(jnp.maximum(values, -bound), bound).astype(held_as)


def setup_inputs(seed: int = 0) -> dict:
    streams_of = jax.random.split(jax.random.key(seed), 9)
    return {
        "temporal_out": noise(streams_of[0], (FRAMES, D), 1.0, 6.0, ((0, 16),)),
        "depth_in": noise(streams_of[1], (CODEBOOKS, D, DD), D ** -0.5, 0.09375, ((0, 8), (1, 16))),
        "embed": noise(streams_of[2], (CODEBOOKS, V, DD), 1.0, 6.0, ((0, 8),)),
        "depth_w1": noise(streams_of[3], (CODEBOOKS, DD, DH), DD ** -0.5, 0.1875, ((0, 8), (2, 16))),
        "depth_w2": noise(streams_of[4], (CODEBOOKS, DD, DH), DH ** -0.5, 0.125, ((0, 8), (2, 16))),
        "audio_tokens": plant(jax.random.randint(streams_of[5], (FRAMES, CODEBOOKS), 0, V), jax.random.fold_in(streams_of[5], 1), 0, V - 1).astype(jnp.int32),
        "barge_mask": plant((jax.random.randint(streams_of[6], (FRAMES,), 0, 2) < 1).astype(jnp.int32), jax.random.fold_in(streams_of[6], 1), 0, 1),
        "out_grad": noise(streams_of[7], (FRAMES, CODEBOOKS, DD), 1.0, 6.0, ((0, 16), (1, 8))),
    }


EPS = 1e-06

def matmul(left, right):
    return jnp.dot(left, right, preferred_element_type=jnp.float32)

def contract_rows(left, right):
    return lax.dot_general(left, right, (((0,), (0,)), ((), ())), preferred_element_type=jnp.float32)

def contract_cols(left, right):
    return lax.dot_general(left, right, (((1,), (1,)), ((), ())), preferred_element_type=jnp.float32)

def silu_slope(values):
    sigma = jax.nn.sigmoid(values)
    return sigma * (1.0 + values * (1.0 - sigma))

def group_sum(left, right):
    total = jnp.zeros((left.shape[1], right.shape[1]), jnp.float32)
    for group in range(N_DP):
        first = group * ROWS_DEV
        part = contract_rows(left[first:first + ROWS_DEV], right[first:first + ROWS_DEV]).astype(jnp.bfloat16)
        total = total + part.astype(jnp.float32)
    return total.astype(jnp.bfloat16)

def reference(temporal_out, depth_in, embed, depth_w1, depth_w2, audio_tokens, barge_mask, out_grad):
    row_weight = barge_mask.astype(jnp.float32)[:, None]
    incoming = jnp.zeros((FRAMES, DD), jnp.bfloat16)
    saved = []
    for book in range(CODEBOOKS):
        table_rows = jnp.take(embed[book], audio_tokens[:, book], axis=0).astype(jnp.float32)
        resid = matmul(temporal_out, depth_in[book]) + table_rows + incoming.astype(jnp.float32)
        scale = lax.rsqrt(lax.optimization_barrier(jnp.mean(resid * resid, axis=-1, keepdims=True)) + EPS)
        normed = (resid * scale).astype(jnp.bfloat16)
        pre_act = matmul(normed, depth_w1[book])
        active = jax.nn.silu(pre_act).astype(jnp.bfloat16)
        incoming = (resid + contract_cols(active, depth_w2[book])).astype(jnp.bfloat16)
        saved.append((resid, scale, normed, pre_act, active))
    vocab_ids = jnp.arange(V, dtype=jnp.int32)[None, :]
    from_next = jnp.zeros((FRAMES, DD), jnp.bfloat16)
    temporal_slope = jnp.zeros((FRAMES, D), jnp.float32)
    w1_list = [None] * CODEBOOKS
    w2_list = [None] * CODEBOOKS
    in_list = [None] * CODEBOOKS
    embed_list = [None] * CODEBOOKS
    for book in reversed(range(CODEBOOKS)):
        resid, scale, normed, pre_act, active = saved[book]
        state_slope = out_grad[:, book, :].astype(jnp.float32) * row_weight + from_next.astype(jnp.float32)
        slope_b = state_slope.astype(jnp.bfloat16)
        pre_slope = (matmul(slope_b, depth_w2[book]) * silu_slope(pre_act)).astype(jnp.bfloat16)
        norm_slope = contract_cols(pre_slope, depth_w1[book])
        unit_rows = resid * scale
        from_next = (state_slope + scale * (norm_slope - unit_rows * lax.optimization_barrier(jnp.mean(norm_slope * unit_rows, axis=-1, keepdims=True)))).astype(jnp.bfloat16)
        w1_list[book] = group_sum(normed, pre_slope)
        w2_list[book] = group_sum(slope_b, active)
        in_list[book] = group_sum(temporal_out, from_next)
        onehot = (audio_tokens[:, book][:, None] == vocab_ids).astype(jnp.bfloat16)
        embed_list[book] = group_sum(onehot, from_next)
        term = contract_cols(from_next, depth_in[book]).astype(jnp.bfloat16)
        temporal_slope = temporal_slope + term.astype(jnp.float32)
    temporal_grad = temporal_slope.astype(jnp.bfloat16)
    return (temporal_grad, jnp.stack(in_list), jnp.stack(embed_list), jnp.stack(w1_list), jnp.stack(w2_list))
```

```python
import functools

import jax
import jax.numpy as jnp
from jax import lax
from jax.experimental import pallas as pl
from jax.experimental.pallas import tpu as pltpu
from jax.sharding import PartitionSpec as P

EPS = 1e-06
F32 = jnp.float32
BF16 = jnp.bfloat16
SUBLANES = 8


def dot_nn(left, right):
    return lax.dot_general(left, right, (((1,), (0,)), ((), ())), preferred_element_type=F32)


def dot_nt(left, right):
    return lax.dot_general(left, right, (((1,), (1,)), ((), ())), preferred_element_type=F32)


def shifted(block, axis, distance):
    devices = range(lax.axis_size(axis))
    route = [(i - distance, i) for i in devices if i - distance in devices]
    return lax.ppermute(block, axis, route)


VMEM = pl.BlockSpec(memory_space=pltpu.VMEM)


def params(megabytes):
    return pltpu.CompilerParams(vmem_limit_bytes=megabytes * 1024 * 1024)


def base_kernel(t_ref, w_ref, emb_ref, out_ref):
    step = pl.program_id(0)

    @pl.when(step == 0)
    def _():
        out_ref[...] = emb_ref[...].astype(F32)

    out_ref[...] += dot_nn(t_ref[...], w_ref[0])


def depth_base(temporal, gathered, token_rows, n_dp, piece):
    rows, _ = temporal.shape
    width = gathered.shape[-1]
    return pl.pallas_call(
        base_kernel,
        grid=(n_dp,),
        in_specs=[
            pl.BlockSpec((rows, piece), lambda s: (0, s)),
            pl.BlockSpec((1, piece, width), lambda s: (s, 0, 0)),
            pl.BlockSpec((rows, width), lambda s: (0, 0)),
        ],
        out_specs=pl.BlockSpec((rows, width), lambda s: (0, 0)),
        out_shape=jax.ShapeDtypeStruct((rows, width), F32),
        cost_estimate=pl.CostEstimate(
            flops=2 * rows * width * piece * n_dp,
            bytes_accessed=2 * width * piece * n_dp,
            transcendentals=0,
        ),
        name="depth_base",
    )(temporal, gathered, token_rows)


def chunk_sizes(hidden):
    size = hidden // 4 if hidden % (4 * SUBLANES) == 0 else hidden
    return [(start, size) for start in range(0, hidden, size)]


def normalise(resid):
    scale = lax.rsqrt(jnp.mean(resid * resid, axis=-1, keepdims=True) + EPS)
    return scale, (resid * scale).astype(BF16)


def forward_kernel(base_ref, in_ref, w1_ref, w2_ref, out_ref):
    resid = base_ref[...] + in_ref[...].astype(F32)
    _, normed = normalise(resid)
    total = resid
    for start, size in chunk_sizes(w1_ref.shape[0]):
        pre = dot_nt(normed, w1_ref[pl.ds(start, size), :])
        active = (pre * jax.nn.sigmoid(pre)).astype(BF16)
        total = total + dot_nn(active, w2_ref[pl.ds(start, size), :])
    out_ref[...] = total.astype(BF16)


def last_forward_kernel(
    base_ref, in_ref, w1_ref, unit_ref, scale_ref, normed_ref, slope_ref, active_ref
):
    resid = base_ref[...] + in_ref[...].astype(F32)
    scale, normed = normalise(resid)
    unit_ref[...] = resid * scale
    scale_ref[...] = scale
    normed_ref[...] = normed
    for start, size in chunk_sizes(w1_ref.shape[0]):
        pre = dot_nt(normed, w1_ref[pl.ds(start, size), :])
        sigma = jax.nn.sigmoid(pre)
        slope_ref[:, pl.ds(start, size)] = sigma * (1.0 + pre * (1.0 - sigma))
        active_ref[pl.ds(start, size), :] = (pre * sigma).astype(BF16).T


def backward_kernel(last, cot_ref, next_ref, w1_ref, w2_ref, unit_ref, scale_ref, slope_ref,
                    carry_ref, *saved):
    state_slope = cot_ref[...] + next_ref[...].astype(F32)
    slope_b = state_slope.astype(BF16)
    norm_slope = jnp.zeros(state_slope.shape, F32)
    for start, size in chunk_sizes(w1_ref.shape[0]):
        hidden = dot_nt(slope_b, w2_ref[pl.ds(start, size), :])
        pre_slope = (hidden * slope_ref[:, pl.ds(start, size)]).astype(BF16)
        if last:
            saved[1][pl.ds(start, size), :] = pre_slope.T
        norm_slope = norm_slope + dot_nn(pre_slope, w1_ref[pl.ds(start, size), :])
    unit = unit_ref[...]
    mean = jnp.mean(norm_slope * unit, axis=-1, keepdims=True)
    carry_ref[...] = (state_slope + scale_ref[...] * (norm_slope - unit * mean)).astype(BF16)
    if last:
        saved[0][...] = slope_b


def turn(kernel, operands, outs, rows, hidden, width, name, passes=2):
    return pl.pallas_call(
        kernel,
        in_specs=[VMEM] * len(operands),
        out_specs=jax.tree.map(lambda _: VMEM, outs),
        out_shape=outs,
        compiler_params=params(40),
        cost_estimate=pl.CostEstimate(
            flops=2 * passes * rows * hidden * width,
            bytes_accessed=2 * passes * hidden * width,
            transcendentals=0,
        ),
        name=name,
    )(*operands)


def term_kernel(c_ref, w_ref, out_ref):
    out_ref[0] = dot_nt(c_ref[...], w_ref[0]).astype(BF16)


def temporal_terms(carried, gathered, n_dp, n_code, piece):
    rows, width = carried.shape
    per = n_dp // n_code
    return pl.pallas_call(
        term_kernel,
        grid=(n_dp,),
        in_specs=[
            pl.BlockSpec((rows, width), lambda s: (0, 0)),
            pl.BlockSpec((1, piece, width), lambda s: (s, 0, 0)),
        ],
        out_specs=pl.BlockSpec((1, rows, piece), lambda s: (s // per, 0, s % per)),
        out_shape=jax.ShapeDtypeStruct((n_code, rows, piece * per), BF16),
        cost_estimate=pl.CostEstimate(
            flops=2 * rows * width * piece * n_dp,
            bytes_accessed=2 * width * piece * n_dp,
            transcendentals=0,
        ),
        name="temporal_terms",
    )(carried, gathered)


def grads_kernel(lc_ref, ls_ref, g_ref, oc_ref, os_ref, ac_ref, as_ref):
    step = pl.program_id(0)
    width = oc_ref.shape[1]

    @pl.when(step == 0)
    def _():
        ac_ref[...] = jnp.zeros_like(ac_ref)
        as_ref[...] = jnp.zeros_like(as_ref)

    ac_ref[...] += dot_nn(lc_ref[...], g_ref[:, :width])
    as_ref[...] += dot_nn(ls_ref[...], g_ref[:, width:])

    @pl.when(step == pl.num_programs(0) - 1)
    def _():
        oc_ref[...] = ac_ref[...].astype(BF16)
        os_ref[...] = as_ref[...].astype(BF16)


def final_grads(left_carry, left_slope, gathered):
    frames, both = gathered.shape
    width = both // 2
    block = 512 if frames % 512 == 0 else frames
    mc, ms = left_carry.shape[0], left_slope.shape[0]
    return pl.pallas_call(
        grads_kernel,
        grid=(frames // block,),
        in_specs=[
            pl.BlockSpec((mc, block), lambda s: (0, s)),
            pl.BlockSpec((ms, block), lambda s: (0, s)),
            pl.BlockSpec((block, both), lambda s: (s, 0)),
        ],
        out_specs=[
            pl.BlockSpec((mc, width), lambda s: (0, 0)),
            pl.BlockSpec((ms, width), lambda s: (0, 0)),
        ],
        out_shape=[
            jax.ShapeDtypeStruct((mc, width), BF16),
            jax.ShapeDtypeStruct((ms, width), BF16),
        ],
        scratch_shapes=[pltpu.VMEM((mc, width), F32), pltpu.VMEM((ms, width), F32)],
        cost_estimate=pl.CostEstimate(
            flops=2 * (mc + ms) * width * frames,
            bytes_accessed=2 * frames * both,
            transcendentals=0,
        ),
        name="final_grads",
    )(left_carry, left_slope, gathered)


def per_device(
    temporal_out, depth_in, embed, depth_w1, depth_w2, audio_tokens, barge_mask, out_grad
):
    dp_index = lax.axis_index("dp")
    n_dp, n_code = lax.axis_size("dp"), lax.axis_size("code")
    rows = temporal_out.shape[0]
    piece, width = depth_in.shape[1:]
    own_hidden = depth_w1.shape[2]
    table = embed[0]

    pad_hidden = -own_hidden % SUBLANES
    held = own_hidden + pad_hidden
    hidden = held * n_dp
    pad = ((0, pad_hidden), (0, 0))
    shard = jnp.concatenate(
        [depth_in[0], jnp.pad(depth_w1[0].T, pad), jnp.pad(depth_w2[0].T, pad)], axis=0
    )
    gathered = lax.all_gather(shard, "dp", axis=0)
    w_first = gathered[:, piece:piece + held].reshape(hidden, width)
    w_second = gathered[:, piece + held:].reshape(hidden, width)

    token_all = audio_tokens[:, 0]
    token_own = lax.dynamic_slice_in_dim(token_all, dp_index * rows, rows, 0)
    token_rows = jnp.take(table, token_own, axis=0)
    base = depth_base(temporal_out, gathered, token_rows, n_dp, piece)
    temporal_all = lax.all_gather(
        lax.optimization_barrier((temporal_out, base))[0], "dp", axis=0, tiled=True
    )

    state_type = jax.ShapeDtypeStruct((rows, width), BF16)
    incoming = jnp.zeros((rows, width), BF16)
    for _ in range(n_code - 1):
        state = turn(
            forward_kernel, (base, incoming, w_first, w_second), state_type,
            rows, hidden, width, "forward_turn",
        )
        incoming = shifted(state, "code", 1)
    unit, scale, normed, slope, active = turn(
        last_forward_kernel, (base, incoming, w_first),
        [
            jax.ShapeDtypeStruct((rows, width), F32),
            jax.ShapeDtypeStruct((rows, 1), F32),
            state_type,
            jax.ShapeDtypeStruct((rows, hidden), F32),
            jax.ShapeDtypeStruct((hidden, rows), BF16),
        ],
        rows, hidden, width, "last_forward_turn", passes=1,
    )
    normed_all = lax.all_gather(normed, "dp", axis=0, tiled=True)

    cotangent = out_grad[:, 0, :].astype(F32) * barge_mask.astype(F32)[:, None]
    from_next = jnp.zeros((rows, width), BF16)
    for step in range(n_code):
        last = step == n_code - 1
        outs = [state_type]
        if last:
            outs += [state_type, jax.ShapeDtypeStruct((hidden, rows), BF16)]
        results = turn(
            functools.partial(backward_kernel, last),
            (cotangent, from_next, w_first, w_second, unit, scale, slope),
            outs, rows, hidden, width, "last_backward_turn" if last else "backward_turn",
        )
        if not last:
            from_next = shifted(results[0], "code", -1)
    carried, slope_b, pre_slope = results

    late = lax.all_gather(
        jnp.concatenate([carried, slope_b], axis=1), "dp", axis=0, tiled=True
    )
    terms = temporal_terms(carried, gathered, n_dp, n_code, piece)
    terms = lax.all_to_all(terms, "code", 0, 0)
    temporal_grad = jnp.sum(terms.astype(F32), axis=0).astype(BF16)

    hidden_rows = jnp.concatenate(
        [active.reshape(n_dp, held, rows), pre_slope.reshape(n_dp, held, rows)], axis=1
    )
    hidden_rows = lax.all_to_all(hidden_rows, "dp", 0, 0)
    hidden_rows = hidden_rows.transpose(1, 0, 2).reshape(2 * held, n_dp * rows)
    active_all, pre_slope_all = hidden_rows[:held], hidden_rows[held:]
    first_grad = dot_nn(pre_slope_all, normed_all).astype(BF16)

    temporal_own = lax.dynamic_slice_in_dim(temporal_all, dp_index * piece, piece, 1).T
    own_vocab = table.shape[0] // n_dp
    vocab_ids = dp_index * own_vocab + lax.broadcasted_iota(jnp.int32, (own_vocab, 1), 0)
    onehot = (token_all[None, :] == vocab_ids).astype(BF16)
    left_carry = jnp.concatenate([temporal_own, onehot], axis=0)
    carry_grads, second_grad = final_grads(left_carry, active_all, late)
    return (
        temporal_grad,
        carry_grads[:piece][None],
        carry_grads[piece:][None],
        first_grad[:own_hidden].T[None],
        second_grad[:own_hidden].T[None],
    )


def solution(mesh):
    in_specs = (
        P("dp", None),
        P("code", "dp", None),
        P("code", None, None),
        P("code", None, "dp"),
        P("code", None, "dp"),
        P(None, "code"),
        P("dp"),
        P("dp", "code", None),
    )
    out_specs = (
        P("dp", "code"),
        P("code", "dp", None),
        P("code", "dp", None),
        P("code", None, "dp"),
        P("code", None, "dp"),
    )
    return jax.shard_map(
        per_device, mesh=mesh, in_specs=in_specs, out_specs=out_specs, check_vma=False
    )
```

```python
import functools

import jax
import jax.numpy as jnp
from jax import lax
from jax.experimental import pallas as pl
from jax.experimental.pallas import tpu as pltpu
from jax.sharding import PartitionSpec as P

EPS = 1e-06
F32 = jnp.float32
BF16 = jnp.bfloat16
SUBLANES = 8


def dot_nn(left, right):
    return lax.dot_general(left, right, (((1,), (0,)), ((), ())), preferred_element_type=F32)


def dot_nt(left, right):
    return lax.dot_general(left, right, (((1,), (1,)), ((), ())), preferred_element_type=F32)


def hop(block, axis, source, target):
    return lax.ppermute(block, axis, [(source, target)])


VMEM = pl.BlockSpec(memory_space=pltpu.VMEM)
ANY = pl.BlockSpec(memory_space=pl.ANY)


def params(megabytes):
    return pltpu.CompilerParams(vmem_limit_bytes=megabytes * 1024 * 1024)


def unpack_kernel(piece, held, t_ref, emb_ref, g_ref, after_ref, base_ref, w1_ref, w2_ref,
                  d_ref, d_sem, w_sem):
    n_dp = g_ref.shape[0]

    def depth_copy(s):
        return pltpu.make_async_copy(
            g_ref.at[s, pl.ds(0, piece)], d_ref.at[pl.ds(s * piece, piece)], d_sem.at[s]
        )

    def weight_copy(s, which):
        to_ref = (w1_ref, w2_ref)[which]
        return pltpu.make_async_copy(
            g_ref.at[s, pl.ds(piece + which * held, held)],
            to_ref.at[pl.ds(s * held, held)],
            w_sem.at[which, s],
        )

    for s in range(n_dp):
        depth_copy(s).start()
    for which in range(2):
        for s in range(n_dp):
            weight_copy(s, which).start()
    base_ref[...] = emb_ref[...].astype(F32)
    group = 4 if n_dp % 4 == 0 else 1
    span = group * piece

    def step(i, _):
        for j in range(group):
            depth_copy(i * group + j).wait()
        start = pl.multiple_of(i * span, span)
        base_ref[...] += dot_nn(t_ref[:, pl.ds(start, span)], d_ref[pl.ds(start, span), :])
        return 0

    lax.fori_loop(0, n_dp // group, step, 0)
    for which in range(2):
        for s in range(n_dp):
            weight_copy(s, which).wait()


def unpack(temporal, token_rows, gathered, after, piece, held):
    rows, _ = temporal.shape
    n_dp, _, width = gathered.shape
    hidden = n_dp * held
    weight = pltpu.VMEM((hidden, width), BF16)
    return pl.pallas_call(
        functools.partial(unpack_kernel, piece, held),
        in_specs=[VMEM, VMEM, pl.BlockSpec(memory_space=pltpu.HBM), ANY],
        out_specs=[VMEM] * 3,
        out_shape=[pltpu.VMEM((rows, width), F32), weight, weight],
        scratch_shapes=[
            pltpu.VMEM((n_dp * piece, width), BF16),
            pltpu.SemaphoreType.DMA((n_dp,)),
            pltpu.SemaphoreType.DMA((2, n_dp)),
        ],
        compiler_params=params(44),
        name="unpack",
    )(temporal, token_rows, gathered, after)


def chunks(hidden):
    return 4 if hidden % (4 * 2 * SUBLANES) == 0 else 1


def normalise(resid):
    scale = lax.rsqrt(jnp.mean(resid * resid, axis=-1, keepdims=True) + EPS)
    return scale, (resid * scale).astype(BF16)


def received(refs, start):
    for ref in refs:
        start = start + ref[...].astype(F32)
    return start


def hidden_loop(hidden, body, init):
    count = chunks(hidden)
    size = hidden // count
    return lax.fori_loop(
        0, count, lambda i, held: body(i, pl.ds(pl.multiple_of(i * size, size), size), held), init
    )


def forward_kernel(turn_index, code_ref, base_ref, w1_ref, w2_ref, *refs):
    out_ref = refs[-1]

    @pl.when(code_ref[0] == turn_index)
    def _():
        resid = received(refs[:-1], base_ref[...])
        _, normed = normalise(resid)

        def body(_, part, total):
            pre = dot_nt(normed, w1_ref[part, :])
            active = (pre * jax.nn.sigmoid(pre)).astype(BF16)
            return total + dot_nn(active, w2_ref[part, :])

        out_ref[...] = hidden_loop(w1_ref.shape[0], body, resid).astype(BF16)


def saved_kernel(base_ref, w1_ref, *refs):
    unit_ref, scale_ref, normed_ref, slope_ref, active_ref = refs[-5:]
    resid = received(refs[:-5], base_ref[...])
    scale, normed = normalise(resid)
    unit_ref[...] = resid * scale
    scale_ref[...] = scale
    normed_ref[...] = normed

    def body(i, part, _):
        pre = dot_nt(normed, w1_ref[part, :])
        sigma = jax.nn.sigmoid(pre)
        slope_ref[i] = sigma * (1.0 + pre * (1.0 - sigma))
        active_ref[part, :] = (pre * sigma).astype(BF16).T
        return 0

    hidden_loop(w1_ref.shape[0], body, 0)


def backward_math(state_slope, w1_ref, w2_ref, unit_ref, scale_ref, slope_ref, keep_ref):
    slope_b = state_slope.astype(BF16)

    def body(i, part, norm_slope):
        hidden = dot_nt(slope_b, w2_ref[part, :])
        pre_slope = (hidden * slope_ref[i]).astype(BF16)
        if keep_ref is not None:
            keep_ref[part, :] = pre_slope.T
        return norm_slope + dot_nn(pre_slope, w1_ref[part, :])

    norm_slope = hidden_loop(w1_ref.shape[0], body, jnp.zeros(state_slope.shape, F32))
    unit = unit_ref[...]
    mean = jnp.mean(norm_slope * unit, axis=-1, keepdims=True)
    carried = state_slope + scale_ref[...] * (norm_slope - unit * mean)
    return carried.astype(BF16), slope_b


def backward_kernel(
    owner, code_ref, cot_ref, w1_ref, w2_ref, unit_ref, scale_ref, slope_ref, *refs
):
    out_ref = refs[-1]

    @pl.when(code_ref[0] == owner)
    def _():
        state_slope = received(refs[:-1], cot_ref[...])
        out_ref[...], _ = backward_math(
            state_slope, w1_ref, w2_ref, unit_ref, scale_ref, slope_ref, None
        )


def last_kernel(cot_ref, w1_ref, w2_ref, unit_ref, scale_ref, slope_ref, *refs):
    late_ref, pre_ref = refs[-2:]
    width = cot_ref.shape[1]
    state_slope = received(refs[:-2], cot_ref[...])
    late_ref[:, :width], late_ref[:, width:] = backward_math(
        state_slope, w1_ref, w2_ref, unit_ref, scale_ref, slope_ref, pre_ref
    )


def turn(kernel, operands, outs, name, sizes):
    rows, hidden, width = sizes
    scalar = [pl.BlockSpec(memory_space=pltpu.SMEM)] if operands[0].dtype == jnp.int32 else []
    return pl.pallas_call(
        kernel,
        in_specs=scalar + [VMEM] * (len(operands) - len(scalar)),
        out_specs=jax.tree.map(lambda _: VMEM, outs),
        out_shape=outs,
        compiler_params=params(10),
        cost_estimate=pl.CostEstimate(
            flops=4 * rows * hidden * width, bytes_accessed=4 * hidden * width, transcendentals=0
        ),
        name=name,
    )(*operands)


def term_kernel(c_ref, w_ref, after_ref, out_ref):
    pieces, piece, width = w_ref.shape
    parts, _, columns = out_ref.shape
    terms = dot_nt(c_ref[...], w_ref[...].reshape(pieces * piece, width)).astype(BF16)
    for part in range(parts):
        out_ref[part] = terms[:, part * columns:(part + 1) * columns]


def temporal_terms(late, gathered, after, n_code, piece):
    rows = late.shape[0]
    n_dp, _, width = gathered.shape
    columns = n_dp * piece // n_code
    steps = 4 if n_dp % 4 == 0 and n_code % 4 == 0 else 1
    return pl.pallas_call(
        term_kernel,
        grid=(steps,),
        in_specs=[
            pl.BlockSpec((rows, width), lambda s: (0, 0)),
            pl.BlockSpec((n_dp // steps, piece, width), lambda s: (s, 0, 0)),
            ANY,
        ],
        out_specs=pl.BlockSpec((n_code // steps, rows, columns), lambda s: (s, 0, 0)),
        out_shape=jax.ShapeDtypeStruct((n_code, rows, columns), BF16),
        compiler_params=params(50),
        cost_estimate=pl.CostEstimate(
            flops=2 * rows * width * piece * n_dp,
            bytes_accessed=2 * width * piece * n_dp,
            transcendentals=0,
        ),
        name="temporal_terms",
    )(late, gathered, after)


def grads_kernel(lt_ref, lo_ref, ls_ref, g_ref, ot_ref, oo_ref, os_ref, at_ref, ao_ref, as_ref):
    step = pl.program_id(0)
    width = ot_ref.shape[1]
    work = ((lt_ref, ot_ref, at_ref, 0), (lo_ref, oo_ref, ao_ref, 0), (ls_ref, os_ref, as_ref, 1))

    @pl.when(step == 0)
    def _():
        for _, _, acc_ref, _ in work:
            acc_ref[...] = jnp.zeros_like(acc_ref)

    for left_ref, _, acc_ref, half in work:
        acc_ref[...] += dot_nn(left_ref[...], g_ref[:, half * width:(half + 1) * width])

    @pl.when(step == pl.num_programs(0) - 1)
    def _():
        for _, out_ref, acc_ref, _ in work:
            out_ref[...] = acc_ref[: out_ref.shape[0], :].astype(BF16)


def final_grads(lefts, out_rows, gathered):
    frames, both = gathered.shape
    width = both // 2
    block = 512 if frames % 512 == 0 else frames
    return pl.pallas_call(
        grads_kernel,
        grid=(frames // block,),
        in_specs=[pl.BlockSpec((left.shape[0], block), lambda s: (0, s)) for left in lefts]
        + [pl.BlockSpec((block, both), lambda s: (s, 0))],
        out_specs=[pl.BlockSpec((rows, width), lambda s: (0, 0)) for rows in out_rows],
        out_shape=[jax.ShapeDtypeStruct((rows, width), BF16) for rows in out_rows],
        scratch_shapes=[pltpu.VMEM((left.shape[0], width), F32) for left in lefts],
        compiler_params=params(58),
        cost_estimate=pl.CostEstimate(
            flops=2 * sum(left.shape[0] for left in lefts) * width * frames,
            bytes_accessed=2 * frames * both,
            transcendentals=0,
        ),
        name="final_grads",
    )(*lefts, gathered)


def per_device(
    temporal_out, depth_in, embed, depth_w1, depth_w2, audio_tokens, barge_mask, out_grad
):
    dp_index = lax.axis_index("dp")
    n_dp, n_code = lax.axis_size("dp"), lax.axis_size("code")
    rows = temporal_out.shape[0]
    piece, width = depth_in.shape[1:]
    own_hidden = depth_w1.shape[2]
    table = embed[0]

    pad_hidden = -own_hidden % SUBLANES
    held = own_hidden + pad_hidden
    hidden = held * n_dp
    pad = ((0, pad_hidden), (0, 0))
    shard = jnp.concatenate(
        [depth_in[0], jnp.pad(depth_w1[0].T, pad), jnp.pad(depth_w2[0].T, pad)], axis=0
    )
    gathered = lax.all_gather(shard, "dp", axis=0)
    token_all = audio_tokens[:, 0]
    token_own = lax.dynamic_slice_in_dim(token_all, dp_index * rows, rows, 0)
    token_rows = jnp.take(table, token_own, axis=0)
    temporal_all = lax.all_to_all(
        temporal_out.T.reshape(n_dp, piece, rows), "dp", 0, 0
    )
    base, w_first, w_second = unpack(
        temporal_out, token_rows, gathered, temporal_all, piece, held
    )

    code = lax.axis_index("code").astype(jnp.int32).reshape(1)
    sizes = (rows, hidden, width)
    state_type = jax.ShapeDtypeStruct((rows, width), BF16)
    got = []
    for step in range(n_code - 1):
        state = turn(
            functools.partial(forward_kernel, step),
            (code, base, w_first, w_second, *got[-1:]),
            state_type, "forward_turn", sizes,
        )
        got.append(hop(state, "code", step, step + 1))
    count = chunks(hidden)
    unit, scale, normed, slope, active = turn(
        saved_kernel,
        (base, w_first, *got),
        [
            jax.ShapeDtypeStruct((rows, width), F32),
            jax.ShapeDtypeStruct((rows, 1), F32),
            state_type,
            jax.ShapeDtypeStruct((count, rows, hidden // count), F32),
            jax.ShapeDtypeStruct((hidden, rows), BF16),
        ],
        "saved_values", sizes,
    )
    normed_all = lax.all_gather(normed, "dp", axis=0, tiled=True)

    cotangent = out_grad[:, 0, :].astype(F32) * barge_mask.astype(F32)[:, None]
    saved = (cotangent, w_first, w_second, unit, scale, slope)
    got = []
    for owner in range(n_code - 1, 0, -1):
        carried = turn(
            functools.partial(backward_kernel, owner), (code, *saved, *got[-1:]),
            state_type, "backward_turn", sizes,
        )
        got.append(hop(carried, "code", owner, owner - 1))
    late, pre_slope = turn(
        last_kernel, (*saved, *got),
        [
            jax.ShapeDtypeStruct((rows, 2 * width), BF16),
            jax.ShapeDtypeStruct((hidden, rows), BF16),
        ],
        "last_values", sizes,
    )

    late_all = lax.all_gather(late, "dp", axis=0, tiled=True)
    hidden_rows = jnp.concatenate(
        [active.reshape(n_dp, held, rows), pre_slope.reshape(n_dp, held, rows)], axis=1
    )
    hidden_rows = lax.all_to_all(hidden_rows, "dp", 0, 0)
    terms = temporal_terms(late, gathered, hidden_rows, n_code, piece)
    terms = lax.all_to_all(terms, "code", 0, 0)
    temporal_grad = jnp.sum(terms.astype(F32), axis=0).astype(BF16)

    hidden_rows = hidden_rows.transpose(1, 0, 2).reshape(2 * held, n_dp * rows)
    active_all, pre_slope_all = hidden_rows[:held], hidden_rows[held:]
    first_grad = dot_nn(pre_slope_all, normed_all).astype(BF16)

    temporal_own = temporal_all.transpose(1, 0, 2).reshape(piece, n_dp * rows)
    own_vocab = table.shape[0] // n_dp
    vocab_ids = dp_index * own_vocab + lax.broadcasted_iota(jnp.int32, (own_vocab, 1), 0)
    onehot = (token_all[None, :] == vocab_ids).astype(BF16)
    in_grad, table_grad, second_grad = final_grads(
        (temporal_own, onehot, active_all), (piece, own_vocab, own_hidden), late_all
    )
    return (
        temporal_grad,
        in_grad[None],
        table_grad[None],
        first_grad[:own_hidden].T[None],
        second_grad.T[None],
    )


def solution(mesh):
    in_specs = (
        P("dp", None),
        P("code", "dp", None),
        P("code", None, None),
        P("code", None, "dp"),
        P("code", None, "dp"),
        P(None, "code"),
        P("dp"),
        P("dp", "code", None),
    )
    out_specs = (
        P("dp", "code"),
        P("code", "dp", None),
        P("code", "dp", None),
        P("code", None, "dp"),
        P("code", None, "dp"),
    )
    return jax.shard_map(
        per_device, mesh=mesh, in_specs=in_specs, out_specs=out_specs, check_vma=False
    )
```

```python
import functools

import jax
import jax.numpy as jnp
from jax import lax
from jax.experimental import pallas as pl
from jax.experimental.pallas import tpu as pltpu
from jax.sharding import PartitionSpec as P

EPS = 1e-06
F32 = jnp.float32
BF16 = jnp.bfloat16
SUBLANES = 8


def dot_nn(left, right):
    return lax.dot_general(left, right, (((1,), (0,)), ((), ())), preferred_element_type=F32)


def dot_nt(left, right):
    return lax.dot_general(left, right, (((1,), (1,)), ((), ())), preferred_element_type=F32)


def hop(block, axis, source, target):
    return lax.ppermute(block, axis, [(source, target)])


VMEM = pl.BlockSpec(memory_space=pltpu.VMEM)
ANY = pl.BlockSpec(memory_space=pl.ANY)
SMEM = pl.BlockSpec(memory_space=pltpu.SMEM)
HBM = pl.BlockSpec(memory_space=pltpu.HBM)
HALVES, CORES = 2, 2


def params(megabytes):
    return pltpu.CompilerParams(vmem_limit_bytes=megabytes * 1024 * 1024)


def add_depth(piece, half_ref, t_ref, start, g_ref, d_ref, d_sem):
    n = g_ref.shape[0]
    span = CORES * piece

    def copy(s):
        return pltpu.make_async_copy(
            g_ref.at[s, pl.ds(0, piece)], d_ref.at[pl.ds(s * piece, piece)], d_sem.at[s]
        )

    for s in range(n):
        copy(s).start()

    def total():
        result = start
        for x in range(n // CORES):
            for core in range(CORES):
                copy(x * CORES + core).wait()
            column = pl.multiple_of((x * HALVES + half_ref[0]) * span, span)
            part = d_ref[pl.ds(x * span, span), :]
            result = result + dot_nn(t_ref[:, pl.ds(column, span)], part)
        return result

    return total


def own_kernel(piece, half_ref, t_ref, start_ref, g_ref, after_ref, base_ref, d_ref, d_sem):
    start = start_ref[...].astype(F32)
    base_ref[...] = add_depth(piece, half_ref, t_ref, start, g_ref, d_ref, d_sem)()


def other_kernel(piece, held, half_ref, t_ref, start_ref, own_ref, g_ref, base_ref, w1_ref,
                 w2_ref, d_ref, d_sem, w_sem):
    n = g_ref.shape[0]
    total = add_depth(piece, half_ref, t_ref, start_ref[...], g_ref, d_ref, d_sem)

    def copy(s, which, part):
        return pltpu.make_async_copy(
            (own_ref, g_ref)[part].at[s, pl.ds(piece + which * held, held)],
            (w1_ref, w2_ref)[which].at[pl.ds((part * n + s) * held, held)],
            w_sem.at[which, part * n + s],
        )

    every = [(s, which, part) for which in range(2) for part in range(2) for s in range(n)]
    for one in every:
        copy(*one).start()
    base_ref[...] = total()
    for one in every:
        copy(*one).wait()


def unpack_own(half, temporal, start, own, after, piece):
    rows, width = start.shape
    n = own.shape[0]
    return pl.pallas_call(
        functools.partial(own_kernel, piece),
        in_specs=[SMEM, VMEM, VMEM, HBM, ANY],
        out_specs=VMEM,
        out_shape=jax.ShapeDtypeStruct((rows, width), F32),
        scratch_shapes=[
            pltpu.VMEM((n * piece, width), BF16),
            pltpu.SemaphoreType.DMA((n,)),
        ],
        compiler_params=params(50),
        name="unpack_own",
    )(half, temporal, start, own, after)


def unpack_other(half, temporal, start, own, other, piece, held):
    rows, width = start.shape
    n = own.shape[0]
    weight = pltpu.VMEM((2 * n * held, width), BF16)
    return pl.pallas_call(
        functools.partial(other_kernel, piece, held),
        in_specs=[SMEM, VMEM, VMEM, HBM, HBM],
        out_specs=[VMEM] * 3,
        out_shape=[pltpu.VMEM((rows, width), F32), weight, weight],
        scratch_shapes=[
            pltpu.VMEM((n * piece, width), BF16),
            pltpu.SemaphoreType.DMA((n,)),
            pltpu.SemaphoreType.DMA((2, 2 * n)),
        ],
        compiler_params=params(44),
        name="unpack_other",
    )(half, temporal, start, own, other)


def normalise(resid):
    scale = lax.rsqrt(jnp.mean(resid * resid, axis=-1, keepdims=True) + EPS)
    return scale, (resid * scale).astype(BF16)


def received(refs, start):
    for ref in refs:
        start = start + ref[...].astype(F32)
    return start


def forward_kernel(turn_index, code_ref, base_ref, w1_ref, w2_ref, *refs):
    out_ref = refs[-1]

    @pl.when(code_ref[0] == turn_index)
    def _():
        resid = received(refs[:-1], base_ref[...])
        _, normed = normalise(resid)
        pre = dot_nt(normed, w1_ref[...])
        active = (pre * jax.nn.sigmoid(pre)).astype(BF16)
        out_ref[...] = (resid + dot_nn(active, w2_ref[...])).astype(BF16)


def saved_kernel(base_ref, w1_ref, *refs):
    unit_ref, scale_ref, normed_ref, slope_ref, active_ref = refs[-5:]
    resid = received(refs[:-5], base_ref[...])
    scale, normed = normalise(resid)
    unit_ref[...] = resid * scale
    scale_ref[...] = scale
    normed_ref[...] = normed
    pre = dot_nt(normed, w1_ref[...])
    sigma = jax.nn.sigmoid(pre)
    slope_ref[...] = sigma * (1.0 + pre * (1.0 - sigma))
    active_ref[...] = (pre * sigma).astype(BF16).T


def backward_math(state_slope, w1_ref, w2_ref, unit_ref, scale_ref, slope_ref, keep_ref):
    slope_b = state_slope.astype(BF16)
    pre_slope = (dot_nt(slope_b, w2_ref[...]) * slope_ref[...]).astype(BF16)
    if keep_ref is not None:
        keep_ref[...] = pre_slope.T
    norm_slope = dot_nn(pre_slope, w1_ref[...])
    unit = unit_ref[...]
    mean = jnp.mean(norm_slope * unit, axis=-1, keepdims=True)
    carried = state_slope + scale_ref[...] * (norm_slope - unit * mean)
    return carried.astype(BF16), slope_b


def backward_kernel(
    owner, code_ref, cot_ref, w1_ref, w2_ref, unit_ref, scale_ref, slope_ref, *refs
):
    out_ref = refs[-1]

    @pl.when(code_ref[0] == owner)
    def _():
        state_slope = received(refs[:-1], cot_ref[...])
        out_ref[...], _ = backward_math(
            state_slope, w1_ref, w2_ref, unit_ref, scale_ref, slope_ref, None
        )


def last_kernel(cot_ref, w1_ref, w2_ref, unit_ref, scale_ref, slope_ref, *refs):
    late_ref, pre_ref = refs[-2:]
    width = cot_ref.shape[1]
    state_slope = received(refs[:-2], cot_ref[...])
    late_ref[:, :width], late_ref[:, width:] = backward_math(
        state_slope, w1_ref, w2_ref, unit_ref, scale_ref, slope_ref, pre_ref
    )


def turn(kernel, operands, outs, name, sizes):
    rows, hidden, width = sizes
    scalar = [SMEM] if operands[0].dtype == jnp.int32 else []
    return pl.pallas_call(
        kernel,
        in_specs=scalar + [VMEM] * (len(operands) - len(scalar)),
        out_specs=jax.tree.map(lambda _: VMEM, outs),
        out_shape=outs,
        compiler_params=params(10),
        cost_estimate=pl.CostEstimate(
            flops=4 * rows * hidden * width, bytes_accessed=4 * hidden * width, transcendentals=0
        ),
        name=name,
    )(*operands)


def term_kernel(half_ref, c_ref, own_ref, other_ref, after_ref, out_ref):
    _, piece, width = own_ref.shape
    for w_ref, half in ((own_ref, half_ref[0]), (other_ref, 1 - half_ref[0])):
        part = w_ref[...].reshape(CORES * piece, width)
        out_ref[half] = dot_nt(c_ref[...], part).astype(BF16)


def temporal_terms(half, late, own, other, after, n_code, piece):
    rows = late.shape[0]
    n, _, width = own.shape
    total = 2 * n * piece
    weight = pl.BlockSpec((CORES, piece, width), lambda x: (x, 0, 0))
    return pl.pallas_call(
        term_kernel,
        grid=(n // CORES,),
        in_specs=[SMEM, pl.BlockSpec((rows, width), lambda x: (0, 0)), weight, weight, ANY],
        out_specs=pl.BlockSpec((HALVES, rows, total // n_code), lambda x: (x, 0, 0)),
        out_shape=jax.ShapeDtypeStruct((n_code, rows, total // n_code), BF16),
        compiler_params=params(54),
        cost_estimate=pl.CostEstimate(
            flops=2 * rows * width * total, bytes_accessed=2 * width * total, transcendentals=0
        ),
        name="temporal_terms",
    )(half, late, own, other, after)


def grads_kernel(n, final, *refs):
    lefts, g_ref = refs[:n], refs[n]
    outs, accs = refs[-2 * n:-n], refs[-n:]
    step = pl.program_id(0)
    width = outs[0].shape[1]

    @pl.when(step == 0)
    def _():
        for i in range(n):
            accs[i][...] = refs[n + 1 + i][...] if final else jnp.zeros_like(accs[i])

    for i in range(n):
        right = g_ref[:, width:] if i == n - 1 else g_ref[:, :width]
        accs[i][...] += dot_nn(lefts[i][...], right)

    @pl.when(step == pl.num_programs(0) - 1)
    def _():
        for i in range(n):
            outs[i][...] = accs[i][: outs[i].shape[0], :].astype(outs[i].dtype)


def row_grads(lefts, gathered, partial, out_rows):
    frames, both = gathered.shape
    width = both // 2
    block = 512 if frames % 512 == 0 else frames
    n = len(lefts)
    final = bool(partial)
    outs = [
        jax.ShapeDtypeStruct((rows, width), BF16 if final else F32)
        for rows in (out_rows if final else [left.shape[0] for left in lefts])
    ]
    whole = lambda shape: pl.BlockSpec(shape, lambda s: (0, 0))
    return pl.pallas_call(
        functools.partial(grads_kernel, n, final),
        grid=(frames // block,),
        in_specs=[pl.BlockSpec((left.shape[0], block), lambda s: (0, s)) for left in lefts]
        + [pl.BlockSpec((block, both), lambda s: (s, 0))]
        + [whole(part.shape) for part in partial],
        out_specs=[whole(out.shape) for out in outs],
        out_shape=outs,
        scratch_shapes=[pltpu.VMEM((left.shape[0], width), F32) for left in lefts],
        compiler_params=params(58),
        cost_estimate=pl.CostEstimate(
            flops=2 * sum(left.shape[0] for left in lefts) * width * frames,
            bytes_accessed=2 * frames * both,
            transcendentals=0,
        ),
        name="row_grads",
    )(*lefts, gathered, *partial)


def own_and_other(array, half):
    split = array.reshape((-1, HALVES, CORES) + array.shape[1:])
    pick = lambda which: lax.dynamic_index_in_dim(split, which, 1, keepdims=False)
    return tuple(
        part.reshape((-1,) + array.shape[1:]) for part in (pick(half), pick(1 - half))
    )


def in_dp_order(both, half):
    own, other = (part.reshape((-1, 1, CORES) + part.shape[1:]) for part in both)
    ordered = jnp.where(
        half == 0,
        jnp.concatenate([own, other], axis=1),
        jnp.concatenate([other, own], axis=1),
    )
    return ordered.reshape((-1,) + ordered.shape[3:])


def gather_halves(block, n_dp):
    groups = [
        [i for i in range(n_dp) if i // CORES % HALVES == half] for half in range(HALVES)
    ]
    other = lax.ppermute(block, "dp", [(i, i ^ CORES) for i in range(n_dp)])
    return tuple(
        lax.all_gather(part, "dp", axis=0, axis_index_groups=groups) for part in (block, other)
    )


def lanes(pieces):
    return pieces.transpose(1, 0, 2).reshape(pieces.shape[1], -1)


def per_device(
    temporal_out, depth_in, embed, depth_w1, depth_w2, audio_tokens, barge_mask, out_grad
):
    dp_index = lax.axis_index("dp")
    n_dp, n_code = lax.axis_size("dp"), lax.axis_size("code")
    rows = temporal_out.shape[0]
    piece, width = depth_in.shape[1:]
    own_hidden = depth_w1.shape[2]
    table = embed[0]

    pad_hidden = -own_hidden % SUBLANES
    held = own_hidden + pad_hidden
    hidden = held * n_dp
    pad = ((0, pad_hidden), (0, 0))
    shard = jnp.concatenate(
        [depth_in[0], jnp.pad(depth_w1[0].T, pad), jnp.pad(depth_w2[0].T, pad)], axis=0
    )
    half = (dp_index // CORES % HALVES).astype(jnp.int32)
    halves = (half.reshape(1), 1 - half.reshape(1))
    gathered = gather_halves(shard, n_dp)

    token_all = audio_tokens[:, 0]
    token_own = lax.dynamic_slice_in_dim(token_all, dp_index * rows, rows, 0)
    token_rows = jnp.take(table, token_own, axis=0)
    temporal_all = lax.all_to_all(temporal_out.T.reshape(n_dp, piece, rows), "dp", 0, 0)
    base = unpack_own(
        halves[0], temporal_out, token_rows, gathered[0], temporal_all, piece
    )
    base, w_first, w_second = unpack_other(
        halves[1], temporal_out, base, *gathered, piece, held
    )

    code = lax.axis_index("code").astype(jnp.int32).reshape(1)
    sizes = (rows, hidden, width)
    state_type = jax.ShapeDtypeStruct((rows, width), BF16)
    got = []
    for step in range(n_code - 1):
        state = turn(
            functools.partial(forward_kernel, step),
            (code, base, w_first, w_second, *got[-1:]),
            state_type, "forward_turn", sizes,
        )
        got.append(hop(state, "code", step, step + 1))
    unit, scale, normed, slope, active = turn(
        saved_kernel,
        (base, w_first, *got),
        [
            jax.ShapeDtypeStruct((rows, width), F32),
            jax.ShapeDtypeStruct((rows, 1), F32),
            state_type,
            jax.ShapeDtypeStruct((rows, hidden), F32),
            jax.ShapeDtypeStruct((hidden, rows), BF16),
        ],
        "saved_values", sizes,
    )
    normed_all = lax.all_gather(normed, "dp", axis=0, tiled=True)

    cotangent = out_grad[:, 0, :].astype(F32) * barge_mask.astype(F32)[:, None]
    saved = (cotangent, w_first, w_second, unit, scale, slope)
    got = []
    for owner in range(n_code - 1, 0, -1):
        carried = turn(
            functools.partial(backward_kernel, owner), (code, *saved, *got[-1:]),
            state_type, "backward_turn", sizes,
        )
        got.append(hop(carried, "code", owner, owner - 1))
    late, pre_slope = turn(
        last_kernel, (*saved, *got),
        [
            jax.ShapeDtypeStruct((rows, 2 * width), BF16),
            jax.ShapeDtypeStruct((hidden, rows), BF16),
        ],
        "last_values", sizes,
    )

    late_all = gather_halves(late, n_dp)
    by_part = (HALVES, n_dp // HALVES, held, rows)
    hidden_pieces = jnp.concatenate([active.reshape(by_part), pre_slope.reshape(by_part)], axis=2)
    hidden_all = lax.all_to_all(in_dp_order(hidden_pieces, half), "dp", 0, 0)
    terms = temporal_terms(halves[0], late, *gathered, hidden_all, n_code, piece)
    terms = lax.all_to_all(terms, "code", 0, 0)
    temporal_grad = jnp.sum(terms.astype(F32), axis=0).astype(BF16)
    first_grad = dot_nn(lanes(hidden_all[:, held:]), normed_all).astype(BF16)

    own_vocab = table.shape[0] // n_dp
    vocab_ids = dp_index * own_vocab + lax.broadcasted_iota(jnp.int32, (own_vocab, 1), 0)
    temporal_parts = own_and_other(temporal_all, half)
    token_parts = own_and_other(token_all.reshape(n_dp, rows), half)
    active_parts = own_and_other(hidden_all[:, :held], half)
    grads = ()
    for part in range(HALVES):
        onehot = (token_parts[part].reshape(1, -1) == vocab_ids).astype(BF16)
        grads = row_grads(
            (lanes(temporal_parts[part]), onehot, lanes(active_parts[part])),
            late_all[part].reshape(-1, 2 * width),
            grads,
            (piece, own_vocab, own_hidden),
        )
    in_grad, table_grad, second_grad = grads
    return (
        temporal_grad,
        in_grad[None],
        table_grad[None],
        first_grad[:own_hidden].T[None],
        second_grad.T[None],
    )


def solution(mesh):
    in_specs = (
        P("dp", None),
        P("code", "dp", None),
        P("code", None, None),
        P("code", None, "dp"),
        P("code", None, "dp"),
        P(None, "code"),
        P("dp"),
        P("dp", "code", None),
    )
    out_specs = (
        P("dp", "code"),
        P("code", "dp", None),
        P("code", "dp", None),
        P("code", None, "dp"),
        P("code", None, "dp"),
    )
    return jax.shard_map(
        per_device, mesh=mesh, in_specs=in_specs, out_specs=out_specs, check_vma=False
    )
```

```python
import functools

import jax
import jax.numpy as jnp
from jax import lax
from jax.experimental import pallas as pl
from jax.experimental.pallas import tpu as pltpu
from jax.sharding import PartitionSpec as P

EPS = 1e-06
F32 = jnp.float32
BF16 = jnp.bfloat16
SUBLANES = 8


def dot_nn(left, right):
    return lax.dot_general(left, right, (((1,), (0,)), ((), ())), preferred_element_type=F32)


def dot_nt(left, right):
    return lax.dot_general(left, right, (((1,), (1,)), ((), ())), preferred_element_type=F32)


def hop(block, axis, source, target):
    return lax.ppermute(block, axis, [(source, target)])


VMEM = pl.BlockSpec(memory_space=pltpu.VMEM)
ANY = pl.BlockSpec(memory_space=pl.ANY)
SMEM = pl.BlockSpec(memory_space=pltpu.SMEM)
HBM = pl.BlockSpec(memory_space=pltpu.HBM)
HALVES, CORES = 2, 2
CROSSING = 192


def params(megabytes):
    return pltpu.CompilerParams(vmem_limit_bytes=megabytes * 1024 * 1024)


def add_depth(piece, half_ref, t_ref, start, sources, d_ref, d_sem):
    n = sources[0][0].shape[0]
    span = CORES * piece

    def copies(s):
        first = 0
        for i, (ref, count) in enumerate(sources):
            yield pltpu.make_async_copy(
                ref.at[s, pl.ds(0, count)],
                d_ref.at[pl.ds(s * piece + first, count)],
                d_sem.at[i, s],
            )
            first += count

    for s in range(n):
        for copy in copies(s):
            copy.start()

    def total():
        result = start
        for x in range(n // CORES):
            for core in range(CORES):
                for copy in copies(x * CORES + core):
                    copy.wait()
            column = pl.multiple_of((x * HALVES + half_ref[0]) * span, span)
            part = d_ref[pl.ds(x * span, span), :]
            result = result + dot_nn(t_ref[:, pl.ds(column, span)], part)
        return result

    return total


def own_kernel(piece, half_ref, t_ref, start_ref, g_ref, base_ref, d_ref, d_sem):
    start = start_ref[...].astype(F32)
    sources = ((g_ref, piece),)
    base_ref[...] = add_depth(piece, half_ref, t_ref, start, sources, d_ref, d_sem)()


def other_kernel(piece, held, crossed, half_ref, t_ref, start_ref, own_ref, g_ref, r_ref,
                 base_ref, w1_ref, w2_ref, d_ref, d_sem, w_sem):
    n = g_ref.shape[0]
    sources = ((r_ref, crossed), (g_ref, piece - crossed))
    total = add_depth(piece, half_ref, t_ref, start_ref[...], sources, d_ref, d_sem)

    def copy(s, which, part):
        ref, first = ((own_ref, piece), (g_ref, piece - crossed))[part]
        return pltpu.make_async_copy(
            ref.at[s, pl.ds(first + which * held, held)],
            (w1_ref, w2_ref)[which].at[pl.ds((part * n + s) * held, held)],
            w_sem.at[which, part * n + s],
        )

    every = [(s, which, part) for which in range(2) for part in range(2) for s in range(n)]
    for one in every:
        copy(*one).start()
    base_ref[...] = total()
    for one in every:
        copy(*one).wait()


def unpack_own(half, temporal, start, own, piece):
    rows, width = start.shape
    n = own.shape[0]
    return pl.pallas_call(
        functools.partial(own_kernel, piece),
        in_specs=[SMEM, VMEM, VMEM, HBM],
        out_specs=VMEM,
        out_shape=jax.ShapeDtypeStruct((rows, width), F32),
        scratch_shapes=[
            pltpu.VMEM((n * piece, width), BF16),
            pltpu.SemaphoreType.DMA((1, n)),
        ],
        compiler_params=params(50),
        name="unpack_own",
    )(half, temporal, start, own)


def unpack_other(half, temporal, start, own, other, crossed, piece, held):
    rows, width = start.shape
    n = own.shape[0]
    weight = pltpu.VMEM((2 * n * held, width), BF16)
    return pl.pallas_call(
        functools.partial(other_kernel, piece, held, crossed.shape[1]),
        in_specs=[SMEM, VMEM, VMEM, HBM, HBM, HBM],
        out_specs=[VMEM] * 3,
        out_shape=[pltpu.VMEM((rows, width), F32), weight, weight],
        scratch_shapes=[
            pltpu.VMEM((n * piece, width), BF16),
            pltpu.SemaphoreType.DMA((2, n)),
            pltpu.SemaphoreType.DMA((2, 2 * n)),
        ],
        compiler_params=params(44),
        name="unpack_other",
    )(half, temporal, start, own, other, crossed)


def normalise(resid):
    scale = lax.rsqrt(jnp.mean(resid * resid, axis=-1, keepdims=True) + EPS)
    return scale, (resid * scale).astype(BF16)


def received(refs, start):
    for ref in refs:
        start = start + ref[...].astype(F32)
    return start


def forward_kernel(turn_index, code_ref, base_ref, w1_ref, w2_ref, *refs):
    out_ref = refs[-1]

    @pl.when(code_ref[0] == turn_index)
    def _():
        resid = received(refs[:-1], base_ref[...])
        _, normed = normalise(resid)
        pre = dot_nt(normed, w1_ref[...])
        active = (pre * jax.nn.sigmoid(pre)).astype(BF16)
        out_ref[...] = (resid + dot_nn(active, w2_ref[...])).astype(BF16)


def saved_kernel(base_ref, w1_ref, *refs):
    unit_ref, scale_ref, normed_ref, slope_ref, active_ref = refs[-5:]
    resid = received(refs[:-5], base_ref[...])
    scale, normed = normalise(resid)
    unit_ref[...] = resid * scale
    scale_ref[...] = scale
    normed_ref[...] = normed
    pre = dot_nt(normed, w1_ref[...])
    sigma = jax.nn.sigmoid(pre)
    slope_ref[...] = sigma * (1.0 + pre * (1.0 - sigma))
    active_ref[...] = (pre * sigma).astype(BF16).T


def backward_math(state_slope, w1_ref, w2_ref, unit_ref, scale_ref, slope_ref, keep_ref):
    slope_b = state_slope.astype(BF16)
    pre_slope = (dot_nt(slope_b, w2_ref[...]) * slope_ref[...]).astype(BF16)
    if keep_ref is not None:
        keep_ref[...] = pre_slope.T
    norm_slope = dot_nn(pre_slope, w1_ref[...])
    unit = unit_ref[...]
    mean = jnp.mean(norm_slope * unit, axis=-1, keepdims=True)
    carried = state_slope + scale_ref[...] * (norm_slope - unit * mean)
    return carried.astype(BF16), slope_b


def backward_kernel(
    owner, n_got, code_ref, cot_ref, w1_ref, w2_ref, unit_ref, scale_ref, slope_ref, *refs
):
    out_ref = refs[-1]

    @pl.when(code_ref[0] == owner)
    def _():
        state_slope = received(refs[:n_got], cot_ref[...])
        out_ref[...], _ = backward_math(
            state_slope, w1_ref, w2_ref, unit_ref, scale_ref, slope_ref, None
        )


def last_kernel(cot_ref, w1_ref, w2_ref, unit_ref, scale_ref, slope_ref, *refs):
    late_ref, pre_ref = refs[-2:]
    width = cot_ref.shape[1]
    state_slope = received(refs[:-2], cot_ref[...])
    late_ref[:, :width], late_ref[:, width:] = backward_math(
        state_slope, w1_ref, w2_ref, unit_ref, scale_ref, slope_ref, pre_ref
    )


def turn(kernel, operands, outs, name, sizes, after=()):
    rows, hidden, width = sizes
    scalar = [SMEM] if operands[0].dtype == jnp.int32 else []
    return pl.pallas_call(
        kernel,
        in_specs=scalar + [VMEM] * (len(operands) - len(scalar)) + [ANY] * len(after),
        out_specs=jax.tree.map(lambda _: VMEM, outs),
        out_shape=outs,
        compiler_params=params(10),
        cost_estimate=pl.CostEstimate(
            flops=4 * rows * hidden * width, bytes_accessed=4 * hidden * width, transcendentals=0
        ),
        name=name,
    )(*operands, *after)


def term_kernel(half_ref, c_ref, own_ref, crossed_ref, other_ref, after_ref, out_ref):
    _, piece, width = own_ref.shape
    own = own_ref[...].reshape(CORES * piece, width)
    parts = [ref[core] for core in range(CORES) for ref in (crossed_ref, other_ref)]
    other = jnp.concatenate(parts, axis=0)
    for part, half in ((own, half_ref[0]), (other, 1 - half_ref[0])):
        out_ref[half] = dot_nt(c_ref[...], part).astype(BF16)


def temporal_terms(half, late, own, crossed, other, after, n_code, piece):
    rows = late.shape[0]
    n, _, width = own.shape
    total = 2 * n * piece
    first = crossed.shape[1]
    weight = lambda count: pl.BlockSpec((CORES, count, width), lambda x: (x, 0, 0))
    return pl.pallas_call(
        term_kernel,
        grid=(n // CORES,),
        in_specs=[
            SMEM,
            pl.BlockSpec((rows, width), lambda x: (0, 0)),
            weight(piece),
            weight(first),
            weight(piece - first),
            ANY,
        ],
        out_specs=pl.BlockSpec((HALVES, rows, total // n_code), lambda x: (x, 0, 0)),
        out_shape=jax.ShapeDtypeStruct((n_code, rows, total // n_code), BF16),
        compiler_params=params(50),
        cost_estimate=pl.CostEstimate(
            flops=2 * rows * width * total, bytes_accessed=2 * width * total, transcendentals=0
        ),
        name="temporal_terms",
    )(half, late, own, crossed, other, after)


def grads_kernel(n, final, *refs):
    lefts, g_ref = refs[:n], refs[n]
    outs, accs = refs[-2 * n:-n], refs[-n:]
    step = pl.program_id(0)
    width = outs[0].shape[1]

    @pl.when(step == 0)
    def _():
        for i in range(n):
            accs[i][...] = refs[n + 1 + i][...] if final else jnp.zeros_like(accs[i])

    for i in range(n):
        right = g_ref[:, width:] if i == n - 1 else g_ref[:, :width]
        accs[i][...] += dot_nn(lefts[i][...], right)

    @pl.when(step == pl.num_programs(0) - 1)
    def _():
        for i in range(n):
            outs[i][...] = accs[i][: outs[i].shape[0], :].astype(outs[i].dtype)


def row_grads(lefts, gathered, partial, out_rows):
    frames, both = gathered.shape
    width = both // 2
    block = 512 if frames % 512 == 0 else frames
    n = len(lefts)
    final = bool(partial)
    outs = [
        jax.ShapeDtypeStruct((rows, width), BF16 if final else F32)
        for rows in (out_rows if final else [left.shape[0] for left in lefts])
    ]
    whole = lambda shape: pl.BlockSpec(shape, lambda s: (0, 0))
    return pl.pallas_call(
        functools.partial(grads_kernel, n, final),
        grid=(frames // block,),
        in_specs=[pl.BlockSpec((left.shape[0], block), lambda s: (0, s)) for left in lefts]
        + [pl.BlockSpec((block, both), lambda s: (s, 0))]
        + [whole(part.shape) for part in partial],
        out_specs=[whole(out.shape) for out in outs],
        out_shape=outs,
        scratch_shapes=[pltpu.VMEM((left.shape[0], width), F32) for left in lefts],
        compiler_params=params(58),
        cost_estimate=pl.CostEstimate(
            flops=2 * sum(left.shape[0] for left in lefts) * width * frames,
            bytes_accessed=2 * frames * both,
            transcendentals=0,
        ),
        name="row_grads",
    )(*lefts, gathered, *partial)


def own_and_other(array, half):
    split = array.reshape((-1, HALVES, CORES) + array.shape[1:])
    pick = lambda which: lax.dynamic_index_in_dim(split, which, 1, keepdims=False)
    return tuple(
        part.reshape((-1,) + array.shape[1:]) for part in (pick(half), pick(1 - half))
    )


def in_dp_order(both, half):
    own, other = (part.reshape((-1, 1, CORES) + part.shape[1:]) for part in both)
    ordered = jnp.where(
        half == 0,
        jnp.concatenate([own, other], axis=1),
        jnp.concatenate([other, own], axis=1),
    )
    return ordered.reshape((-1,) + ordered.shape[3:])


def swap_halves(block, n_dp):
    return lax.ppermute(block, "dp", [(i, i ^ CORES) for i in range(n_dp)])


def gather_half(block, n_dp):
    groups = [
        [i for i in range(n_dp) if i // CORES % HALVES == half] for half in range(HALVES)
    ]
    return lax.all_gather(block, "dp", axis=0, axis_index_groups=groups)


def exchanged(when, array):
    return lax.cond(when, lambda a: lax.all_to_all(a, "dp", 0, 0), lambda a: a, array)


def lanes(pieces):
    return pieces.transpose(1, 0, 2).reshape(pieces.shape[1], -1)


def per_device(
    temporal_out, depth_in, embed, depth_w1, depth_w2, audio_tokens, barge_mask, out_grad
):
    dp_index = lax.axis_index("dp")
    n_dp, n_code = lax.axis_size("dp"), lax.axis_size("code")
    rows = temporal_out.shape[0]
    piece, width = depth_in.shape[1:]
    own_hidden = depth_w1.shape[2]
    table = embed[0]

    pad_hidden = -own_hidden % SUBLANES
    held = own_hidden + pad_hidden
    hidden = held * n_dp
    pad = ((0, pad_hidden), (0, 0))
    shard = jnp.concatenate(
        [depth_in[0], jnp.pad(depth_w1[0].T, pad), jnp.pad(depth_w2[0].T, pad)], axis=0
    )
    half = (dp_index // CORES % HALVES).astype(jnp.int32)
    halves = (half.reshape(1), 1 - half.reshape(1))
    crossing = CROSSING if piece > CROSSING else piece // 2
    own_shards = gather_half(shard, n_dp)
    other_shards = gather_half(swap_halves(shard[crossing:], n_dp), n_dp)
    crossed = swap_halves(own_shards[:, :crossing], n_dp)

    token_all = audio_tokens[:, 0]
    token_own = lax.dynamic_slice_in_dim(token_all, dp_index * rows, rows, 0)
    token_rows = jnp.take(table, token_own, axis=0)
    base = unpack_own(halves[0], temporal_out, token_rows, own_shards, piece)
    base, w_first, w_second = unpack_other(
        halves[1], temporal_out, base, own_shards, other_shards, crossed, piece, held
    )

    code_index = lax.axis_index("code")
    code = code_index.astype(jnp.int32).reshape(1)
    upper = code_index >= n_code // 2
    temporal_pieces = temporal_out.T.reshape(n_dp, piece, rows)
    sizes = (rows, hidden, width)
    state_type = jax.ShapeDtypeStruct((rows, width), BF16)
    got = []
    for step in range(n_code - 1):
        state = turn(
            functools.partial(forward_kernel, step),
            (code, base, w_first, w_second, *got[-1:]),
            state_type, "forward_turn", sizes,
        )
        got.append(hop(state, "code", step, step + 1))
    unit, scale, normed, slope, active = turn(
        saved_kernel,
        (base, w_first, *got),
        [
            jax.ShapeDtypeStruct((rows, width), F32),
            jax.ShapeDtypeStruct((rows, 1), F32),
            state_type,
            jax.ShapeDtypeStruct((rows, hidden), F32),
            jax.ShapeDtypeStruct((hidden, rows), BF16),
        ],
        "saved_values", sizes,
    )
    normed_all = lax.all_gather(normed, "dp", axis=0, tiled=True)

    by_part = (HALVES, n_dp // HALVES, held, rows)
    active_pieces = in_dp_order(active.reshape(by_part), half)
    early = exchanged(
        jnp.logical_not(upper), jnp.concatenate([temporal_pieces, active_pieces], axis=1)
    )

    cotangent = out_grad[:, 0, :].astype(F32) * barge_mask.astype(F32)[:, None]
    saved = (cotangent, w_first, w_second, unit, scale, slope)
    got = []
    for owner in range(n_code - 1, 0, -1):
        carried = turn(
            functools.partial(backward_kernel, owner, len(got[-1:])),
            (code, *saved, *got[-1:]),
            state_type, "backward_turn", sizes, () if got else (early,),
        )
        got.append(hop(carried, "code", owner, owner - 1))
    late, pre_slope = turn(
        last_kernel, (*saved, *got),
        [
            jax.ShapeDtypeStruct((rows, 2 * width), BF16),
            jax.ShapeDtypeStruct((hidden, rows), BF16),
        ],
        "last_values", sizes,
    )

    late_all = (gather_half(late, n_dp), gather_half(swap_halves(late, n_dp), n_dp))
    early = exchanged(upper, early)
    temporal_all, active_all = early[:, :piece], early[:, piece:]
    pre_all = lax.all_to_all(in_dp_order(pre_slope.reshape(by_part), half), "dp", 0, 0)
    terms = temporal_terms(
        halves[0], late, own_shards, crossed, other_shards, pre_all, n_code, piece
    )
    terms = lax.all_to_all(terms, "code", 0, 0)
    temporal_grad = jnp.sum(terms.astype(F32), axis=0).astype(BF16)
    first_grad = dot_nn(lanes(pre_all), normed_all).astype(BF16)

    own_vocab = table.shape[0] // n_dp
    vocab_ids = dp_index * own_vocab + lax.broadcasted_iota(jnp.int32, (own_vocab, 1), 0)
    temporal_parts = own_and_other(temporal_all, half)
    token_parts = own_and_other(token_all.reshape(n_dp, rows), half)
    active_parts = own_and_other(active_all, half)
    grads = ()
    for part in range(HALVES):
        onehot = (token_parts[part].reshape(1, -1) == vocab_ids).astype(BF16)
        grads = row_grads(
            (lanes(temporal_parts[part]), onehot, lanes(active_parts[part])),
            late_all[part].reshape(-1, 2 * width),
            grads,
            (piece, own_vocab, own_hidden),
        )
    in_grad, table_grad, second_grad = grads
    return (
        temporal_grad,
        in_grad[None],
        table_grad[None],
        first_grad[:own_hidden].T[None],
        second_grad.T[None],
    )


def solution(mesh):
    in_specs = (
        P("dp", None),
        P("code", "dp", None),
        P("code", None, None),
        P("code", None, "dp"),
        P("code", None, "dp"),
        P(None, "code"),
        P("dp"),
        P("dp", "code", None),
    )
    out_specs = (
        P("dp", "code"),
        P("code", "dp", None),
        P("code", "dp", None),
        P("code", None, "dp"),
        P("code", None, "dp"),
    )
    return jax.shard_map(
        per_device, mesh=mesh, in_specs=in_specs, out_specs=out_specs, check_vma=False
    )
```

```python
import functools

import jax
import jax.numpy as jnp
from jax import lax
from jax.experimental import pallas as pl
from jax.experimental.pallas import tpu as pltpu
from jax.sharding import PartitionSpec as P

EPS = 1e-06
F32 = jnp.float32
BF16 = jnp.bfloat16
SUBLANES = 8


def dot_nn(left, right):
    return lax.dot_general(left, right, (((1,), (0,)), ((), ())), preferred_element_type=F32)


def dot_nt(left, right):
    return lax.dot_general(left, right, (((1,), (1,)), ((), ())), preferred_element_type=F32)


def hop(block, axis, source, target):
    return lax.ppermute(block, axis, [(source, target)])


VMEM = pl.BlockSpec(memory_space=pltpu.VMEM)
ANY = pl.BlockSpec(memory_space=pl.ANY)
SMEM = pl.BlockSpec(memory_space=pltpu.SMEM)
HBM = pl.BlockSpec(memory_space=pltpu.HBM)
HALVES, CORES = 2, 2
CROSSING = 96


def params(megabytes):
    return pltpu.CompilerParams(vmem_limit_bytes=megabytes * 1024 * 1024)


def add_depth(piece, half_ref, t_ref, start, sources, d_ref, d_sem):
    n = sources[0][0].shape[0]
    span = CORES * piece

    def copies(s):
        first = 0
        for i, (ref, count) in enumerate(sources):
            yield pltpu.make_async_copy(
                ref.at[s, pl.ds(0, count)],
                d_ref.at[pl.ds(s * piece + first, count)],
                d_sem.at[i, s],
            )
            first += count

    for s in range(n):
        for copy in copies(s):
            copy.start()

    def total():
        result = start
        for x in range(n // CORES):
            for core in range(CORES):
                for copy in copies(x * CORES + core):
                    copy.wait()
            column = pl.multiple_of((x * HALVES + half_ref[0]) * span, span)
            part = d_ref[pl.ds(x * span, span), :]
            result = result + dot_nn(t_ref[:, pl.ds(column, span)], part)
        return result

    return total


def weight_copies(ref, first, held, part, w1_ref, w2_ref, w_sem):
    n = ref.shape[0]
    return [
        pltpu.make_async_copy(
            ref.at[s, pl.ds(first + which * held, held)],
            to_ref.at[pl.ds((part * n + s) * held, held)],
            w_sem.at[which, s],
        )
        for which, to_ref in enumerate((w1_ref, w2_ref))
        for s in range(n)
    ]


def own_kernel(piece, half_ref, t_ref, start_ref, g_ref, after_ref, base_ref, d_ref, d_sem):
    start = start_ref[...].astype(F32)
    sources = ((g_ref, piece),)
    base_ref[...] = add_depth(piece, half_ref, t_ref, start, sources, d_ref, d_sem)()


def other_kernel(piece, held, crossed, half_ref, t_ref, start_ref, own_ref, r_ref, g_ref,
                 base_ref, w1_ref, w2_ref, d_ref, d_sem, w_sem):
    rest = piece - crossed
    sources = ((r_ref, crossed), (g_ref, rest))
    total = add_depth(piece, half_ref, t_ref, start_ref[...], sources, d_ref, d_sem)
    copies = [
        copy
        for part, (ref, first) in enumerate(((own_ref, piece), (g_ref, rest)))
        for copy in weight_copies(ref, first, held, part, w1_ref, w2_ref, w_sem.at[part])
    ]
    for copy in copies:
        copy.start()
    base_ref[...] = total()
    for copy in copies:
        copy.wait()


def unpack_own(half, temporal, start, own, after, piece):
    rows, width = start.shape
    n = own.shape[0]
    return pl.pallas_call(
        functools.partial(own_kernel, piece),
        in_specs=[SMEM, VMEM, VMEM, HBM, ANY],
        out_specs=VMEM,
        out_shape=jax.ShapeDtypeStruct((rows, width), F32),
        scratch_shapes=[
            pltpu.VMEM((n * piece, width), BF16),
            pltpu.SemaphoreType.DMA((1, n)),
        ],
        compiler_params=params(50),
        name="unpack_own",
    )(half, temporal, start, own, after)


def unpack_other(half, temporal, start, own, crossed, other, piece, held):
    rows, width = start.shape
    n = own.shape[0]
    weight = pltpu.VMEM((HALVES * n * held, width), BF16)
    return pl.pallas_call(
        functools.partial(other_kernel, piece, held, crossed.shape[1]),
        in_specs=[SMEM, VMEM, VMEM, HBM, HBM, HBM],
        out_specs=[VMEM] * 3,
        out_shape=[pltpu.VMEM((rows, width), F32), weight, weight],
        scratch_shapes=[
            pltpu.VMEM((n * piece, width), BF16),
            pltpu.SemaphoreType.DMA((2, n)),
            pltpu.SemaphoreType.DMA((HALVES, 2, n)),
        ],
        compiler_params=params(44),
        name="unpack_other",
    )(half, temporal, start, own, crossed, other)


def normalise(resid):
    scale = lax.rsqrt(jnp.mean(resid * resid, axis=-1, keepdims=True) + EPS)
    return scale, (resid * scale).astype(BF16)


def received(refs, start):
    for ref in refs:
        start = start + ref[...].astype(F32)
    return start


def forward_kernel(turn_index, code_ref, base_ref, w1_ref, w2_ref, *refs):
    out_ref = refs[-1]

    @pl.when(code_ref[0] == turn_index)
    def _():
        resid = received(refs[:-1], base_ref[...])
        _, normed = normalise(resid)
        pre = dot_nt(normed, w1_ref[...])
        active = (pre * jax.nn.sigmoid(pre)).astype(BF16)
        out_ref[...] = (resid + dot_nn(active, w2_ref[...])).astype(BF16)


def saved_kernel(base_ref, w1_ref, *refs):
    unit_ref, scale_ref, normed_ref, slope_ref, active_ref = refs[-5:]
    resid = received(refs[:-5], base_ref[...])
    scale, normed = normalise(resid)
    unit_ref[...] = resid * scale
    scale_ref[...] = scale
    normed_ref[...] = normed
    pre = dot_nt(normed, w1_ref[...])
    sigma = jax.nn.sigmoid(pre)
    slope_ref[...] = sigma * (1.0 + pre * (1.0 - sigma))
    active_ref[...] = (pre * sigma).astype(BF16).T


def backward_math(state_slope, w1_ref, w2_ref, unit_ref, scale_ref, slope_ref, keep_ref):
    slope_b = state_slope.astype(BF16)
    pre_slope = (dot_nt(slope_b, w2_ref[...]) * slope_ref[...]).astype(BF16)
    if keep_ref is not None:
        keep_ref[...] = pre_slope.T
    norm_slope = dot_nn(pre_slope, w1_ref[...])
    unit = unit_ref[...]
    mean = jnp.mean(norm_slope * unit, axis=-1, keepdims=True)
    carried = state_slope + scale_ref[...] * (norm_slope - unit * mean)
    return carried.astype(BF16), slope_b


def backward_kernel(
    owner, n_got, code_ref, cot_ref, w1_ref, w2_ref, unit_ref, scale_ref, slope_ref, *refs
):
    out_ref = refs[-1]

    @pl.when(code_ref[0] == owner)
    def _():
        state_slope = received(refs[:n_got], cot_ref[...])
        out_ref[...], _ = backward_math(
            state_slope, w1_ref, w2_ref, unit_ref, scale_ref, slope_ref, None
        )


def last_kernel(cot_ref, w1_ref, w2_ref, unit_ref, scale_ref, slope_ref, *refs):
    late_ref, pre_ref = refs[-2:]
    width = cot_ref.shape[1]
    state_slope = received(refs[:-2], cot_ref[...])
    late_ref[:, :width], late_ref[:, width:] = backward_math(
        state_slope, w1_ref, w2_ref, unit_ref, scale_ref, slope_ref, pre_ref
    )


def turn(kernel, operands, outs, name, sizes, after=()):
    rows, hidden, width = sizes
    scalar = [SMEM] if operands[0].dtype == jnp.int32 else []
    return pl.pallas_call(
        kernel,
        in_specs=scalar + [VMEM] * (len(operands) - len(scalar)) + [ANY] * len(after),
        out_specs=[VMEM] * len(outs) if isinstance(outs, list) else VMEM,
        out_shape=outs,
        compiler_params=params(10),
        cost_estimate=pl.CostEstimate(
            flops=4 * rows * hidden * width, bytes_accessed=4 * hidden * width, transcendentals=0
        ),
        name=name,
    )(*operands, *after)


def term_kernel(half_ref, c_ref, own_ref, crossed_ref, other_ref, out_ref):
    _, piece, width = own_ref.shape
    own = own_ref[...].reshape(CORES * piece, width)
    parts = [ref[core] for core in range(CORES) for ref in (crossed_ref, other_ref)]
    other = jnp.concatenate(parts, axis=0)
    for part, half in ((own, half_ref[0]), (other, 1 - half_ref[0])):
        out_ref[half] = dot_nt(c_ref[...], part).astype(BF16)


def temporal_terms(half, late, own, crossed, other, n_code, piece):
    rows = late.shape[0]
    n, _, width = own.shape
    total = 2 * n * piece
    first = crossed.shape[1]
    weight = lambda count: pl.BlockSpec((CORES, count, width), lambda x: (x, 0, 0))
    return pl.pallas_call(
        term_kernel,
        grid=(n // CORES,),
        in_specs=[
            SMEM,
            pl.BlockSpec((rows, width), lambda x: (0, 0)),
            weight(piece),
            weight(first),
            weight(piece - first),
        ],
        out_specs=pl.BlockSpec((HALVES, rows, total // n_code), lambda x: (x, 0, 0)),
        out_shape=jax.ShapeDtypeStruct((n_code, rows, total // n_code), BF16),
        compiler_params=params(50),
        cost_estimate=pl.CostEstimate(
            flops=2 * rows * width * total, bytes_accessed=2 * width * total, transcendentals=0
        ),
        name="temporal_terms",
    )(half, late, own, crossed, other)


def grads_kernel(n, final, *refs):
    lefts, g_ref = refs[:n], refs[n]
    outs, accs = refs[-2 * n:-n], refs[-n:]
    step = pl.program_id(0)
    width = outs[0].shape[1]

    @pl.when(step == 0)
    def _():
        for i in range(n):
            accs[i][...] = refs[n + 1 + i][...] if final else jnp.zeros_like(accs[i])

    for i in range(n):
        right = g_ref[:, width:] if i == n - 1 else g_ref[:, :width]
        accs[i][...] += dot_nn(lefts[i][...], right)

    @pl.when(step == pl.num_programs(0) - 1)
    def _():
        for i in range(n):
            outs[i][...] = accs[i][: outs[i].shape[0], :].astype(outs[i].dtype)


def row_grads(lefts, gathered, partial, out_rows):
    frames, both = gathered.shape
    width = both // 2
    block = 512 if frames % 512 == 0 else frames
    n = len(lefts)
    final = bool(partial)
    outs = [
        jax.ShapeDtypeStruct((rows, width), BF16 if final else F32)
        for rows in (out_rows if final else [left.shape[0] for left in lefts])
    ]
    whole = lambda shape: pl.BlockSpec(shape, lambda s: (0, 0))
    return pl.pallas_call(
        functools.partial(grads_kernel, n, final),
        grid=(frames // block,),
        in_specs=[pl.BlockSpec((left.shape[0], block), lambda s: (0, s)) for left in lefts]
        + [pl.BlockSpec((block, both), lambda s: (s, 0))]
        + [whole(part.shape) for part in partial],
        out_specs=[whole(out.shape) for out in outs],
        out_shape=outs,
        scratch_shapes=[pltpu.VMEM((left.shape[0], width), F32) for left in lefts],
        compiler_params=params(58),
        cost_estimate=pl.CostEstimate(
            flops=2 * sum(left.shape[0] for left in lefts) * width * frames,
            bytes_accessed=2 * frames * both,
            transcendentals=0,
        ),
        name="row_grads",
    )(*lefts, gathered, *partial)


def own_and_other(array, half):
    split = array.reshape((-1, HALVES, CORES) + array.shape[1:])
    pick = lambda which: lax.dynamic_index_in_dim(split, which, 1, keepdims=False)
    return tuple(
        part.reshape((-1,) + array.shape[1:]) for part in (pick(half), pick(1 - half))
    )


def in_dp_order(both, half):
    own, other = (part.reshape((-1, 1, CORES) + part.shape[1:]) for part in both)
    ordered = jnp.where(
        half == 0,
        jnp.concatenate([own, other], axis=1),
        jnp.concatenate([other, own], axis=1),
    )
    return ordered.reshape((-1,) + ordered.shape[3:])


def swap_halves(block, n_dp):
    return lax.ppermute(block, "dp", [(i, i ^ CORES) for i in range(n_dp)])


def gather_half(block, n_dp):
    groups = [
        [i for i in range(n_dp) if i // CORES % HALVES == half] for half in range(HALVES)
    ]
    return lax.all_gather(block, "dp", axis=0, axis_index_groups=groups)


def lanes(pieces):
    return pieces.transpose(1, 0, 2).reshape(pieces.shape[1], -1)


def per_device(
    temporal_out, depth_in, embed, depth_w1, depth_w2, audio_tokens, barge_mask, out_grad
):
    dp_index = lax.axis_index("dp")
    n_dp, n_code = lax.axis_size("dp"), lax.axis_size("code")
    rows = temporal_out.shape[0]
    piece, width = depth_in.shape[1:]
    own_hidden = depth_w1.shape[2]
    table = embed[0]

    pad_hidden = -own_hidden % SUBLANES
    held = own_hidden + pad_hidden
    hidden = held * n_dp
    pad = ((0, pad_hidden), (0, 0))
    shard = jnp.concatenate(
        [depth_in[0], jnp.pad(depth_w1[0].T, pad), jnp.pad(depth_w2[0].T, pad)], axis=0
    )
    half = (dp_index // CORES % HALVES).astype(jnp.int32)
    halves = (half.reshape(1), 1 - half.reshape(1))
    crossing = CROSSING if piece > CROSSING else piece // 2
    own_shards = gather_half(shard, n_dp)
    other_shards = gather_half(swap_halves(shard[crossing:], n_dp), n_dp)
    crossed = swap_halves(own_shards[:, :crossing], n_dp)

    token_all = audio_tokens[:, 0]
    token_own = lax.dynamic_slice_in_dim(token_all, dp_index * rows, rows, 0)
    token_rows = jnp.take(table, token_own, axis=0)
    temporal_pieces = temporal_out.T.reshape(n_dp, piece, rows)
    base = unpack_own(
        halves[0], temporal_out, token_rows, own_shards, temporal_pieces, piece
    )
    base, w_first, w_second = unpack_other(
        halves[1], temporal_out, base, own_shards, crossed, other_shards, piece, held
    )

    code_index = lax.axis_index("code")
    code = code_index.astype(jnp.int32).reshape(1)
    upper = code_index >= n_code // 2
    sizes = (rows, hidden, width)
    state_type = jax.ShapeDtypeStruct((rows, width), BF16)
    got = []
    for step in range(n_code - 1):
        state = turn(
            functools.partial(forward_kernel, step),
            (code, base, w_first, w_second, *got[-1:]),
            state_type, "forward_turn", sizes,
        )
        got.append(hop(state, "code", step, step + 1))
    unit, scale, normed, slope, active = turn(
        saved_kernel,
        (base, w_first, *got),
        [
            jax.ShapeDtypeStruct((rows, width), F32),
            jax.ShapeDtypeStruct((rows, 1), F32),
            state_type,
            jax.ShapeDtypeStruct((rows, hidden), F32),
            jax.ShapeDtypeStruct((hidden, rows), BF16),
        ],
        "saved_values", sizes,
    )
    normed_all = lax.all_gather(normed, "dp", axis=0, tiled=True)

    by_part = (HALVES, n_dp // HALVES, held, rows)

    def exchanged(_, temporal, active):
        pieces = in_dp_order(active.reshape(by_part), half)
        return lax.all_to_all(jnp.concatenate([temporal, pieces], axis=1), "dp", 0, 0)

    early = jnp.zeros((n_dp, piece + held, rows), BF16)
    early = lax.cond(
        upper, lambda given, *_: given, exchanged, early, temporal_pieces, active
    )

    cotangent = out_grad[:, 0, :].astype(F32) * barge_mask.astype(F32)[:, None]
    saved = (cotangent, w_first, w_second, unit, scale, slope)
    got = []
    for owner in range(n_code - 1, 0, -1):
        carried = turn(
            functools.partial(backward_kernel, owner, len(got[-1:])),
            (code, *saved, *got[-1:]),
            state_type, "backward_turn", sizes, () if got else (early,),
        )
        got.append(hop(carried, "code", owner, owner - 1))
    late, pre_slope = turn(
        last_kernel, (*saved, *got),
        [
            jax.ShapeDtypeStruct((rows, 2 * width), BF16),
            jax.ShapeDtypeStruct((hidden, rows), BF16),
        ],
        "last_values", sizes,
    )

    late_all = (gather_half(late, n_dp), gather_half(swap_halves(late, n_dp), n_dp))
    early = lax.cond(
        upper, exchanged, lambda given, *_: given, early, temporal_pieces, active
    )
    temporal_all, active_all = early[:, :piece], early[:, piece:]
    pre_all = lax.all_to_all(in_dp_order(pre_slope.reshape(by_part), half), "dp", 0, 0)
    terms = temporal_terms(
        halves[0], late, own_shards, crossed, other_shards, n_code, piece
    )
    terms, pre_all = lax.optimization_barrier((terms, pre_all))
    terms = lax.all_to_all(terms, "code", 0, 0)
    temporal_grad = jnp.sum(terms.astype(F32), axis=0).astype(BF16)
    first_grad = dot_nn(lanes(pre_all), normed_all).astype(BF16)

    own_vocab = table.shape[0] // n_dp
    vocab_ids = dp_index * own_vocab + lax.broadcasted_iota(jnp.int32, (own_vocab, 1), 0)
    temporal_parts = own_and_other(temporal_all, half)
    token_parts = own_and_other(token_all.reshape(n_dp, rows), half)
    active_parts = own_and_other(active_all, half)
    grads = ()
    for part in range(HALVES):
        onehot = (token_parts[part].reshape(1, -1) == vocab_ids).astype(BF16)
        grads = row_grads(
            (lanes(temporal_parts[part]), onehot, lanes(active_parts[part])),
            late_all[part].reshape(-1, 2 * width),
            grads,
            (piece, own_vocab, own_hidden),
        )
    in_grad, table_grad, second_grad = grads
    return (
        temporal_grad,
        in_grad[None],
        table_grad[None],
        first_grad[:own_hidden].T[None],
        second_grad.T[None],
    )


def solution(mesh):
    in_specs = (
        P("dp", None),
        P("code", "dp", None),
        P("code", None, None),
        P("code", None, "dp"),
        P("code", None, "dp"),
        P(None, "code"),
        P("dp"),
        P("dp", "code", None),
    )
    out_specs = (
        P("dp", "code"),
        P("code", "dp", None),
        P("code", "dp", None),
        P("code", None, "dp"),
        P("code", None, "dp"),
    )
    return jax.shard_map(
        per_device, mesh=mesh, in_specs=in_specs, out_specs=out_specs, check_vma=False
    )
```

```python
import functools

import jax
import jax.numpy as jnp
from jax import lax
from jax.experimental import pallas as pl
from jax.experimental.pallas import tpu as pltpu
from jax.sharding import PartitionSpec as P

EPS = 1e-06
F32 = jnp.float32
BF16 = jnp.bfloat16
SUBLANES = 8


def dot_nn(left, right):
    return lax.dot_general(left, right, (((1,), (0,)), ((), ())), preferred_element_type=F32)


def dot_nt(left, right):
    return lax.dot_general(left, right, (((1,), (1,)), ((), ())), preferred_element_type=F32)


def hop(block, axis, source, target):
    return lax.ppermute(block, axis, [(source, target)])


VMEM = pl.BlockSpec(memory_space=pltpu.VMEM)
ANY = pl.BlockSpec(memory_space=pl.ANY)
SMEM = pl.BlockSpec(memory_space=pltpu.SMEM)
HBM = pl.BlockSpec(memory_space=pltpu.HBM)
HALVES, CORES = 2, 2
CROSSING = 96


def params(megabytes):
    return pltpu.CompilerParams(vmem_limit_bytes=megabytes * 1024 * 1024)


def add_depth(piece, half_ref, t_ref, start, sources, d_ref, d_sem):
    n = sources[0][0].shape[0]
    span = CORES * piece

    def copies(s):
        first = 0
        for i, (ref, count) in enumerate(sources):
            yield pltpu.make_async_copy(
                ref.at[s, pl.ds(0, count)],
                d_ref.at[pl.ds(s * piece + first, count)],
                d_sem.at[i, s],
            )
            first += count

    for s in range(n):
        for copy in copies(s):
            copy.start()

    def total():
        result = start
        for x in range(n // CORES):
            for core in range(CORES):
                for copy in copies(x * CORES + core):
                    copy.wait()
            column = pl.multiple_of((x * HALVES + half_ref[0]) * span, span)
            part = d_ref[pl.ds(x * span, span), :]
            result = result + dot_nn(t_ref[:, pl.ds(column, span)], part)
        return result

    return total


def weight_copies(ref, first, held, part, w1_ref, w2_ref, w_sem):
    n = ref.shape[0]
    return [
        pltpu.make_async_copy(
            ref.at[s, pl.ds(first + which * held, held)],
            to_ref.at[pl.ds((part * n + s) * held, held)],
            w_sem.at[which, s],
        )
        for which, to_ref in enumerate((w1_ref, w2_ref))
        for s in range(n)
    ]


def own_kernel(piece, half_ref, t_ref, start_ref, g_ref, after_ref, base_ref, d_ref, d_sem):
    start = start_ref[...].astype(F32)
    sources = ((g_ref, piece),)
    base_ref[...] = add_depth(piece, half_ref, t_ref, start, sources, d_ref, d_sem)()


def other_kernel(piece, held, crossed, half_ref, t_ref, start_ref, own_ref, r_ref, g_ref,
                 base_ref, w1_ref, w2_ref, d_ref, d_sem, w_sem):
    rest = piece - crossed
    sources = ((r_ref, crossed), (g_ref, rest))
    total = add_depth(piece, half_ref, t_ref, start_ref[...], sources, d_ref, d_sem)
    copies = [
        copy
        for part, (ref, first) in enumerate(((own_ref, piece), (g_ref, rest)))
        for copy in weight_copies(ref, first, held, part, w1_ref, w2_ref, w_sem.at[part])
    ]
    for copy in copies:
        copy.start()
    base_ref[...] = total()
    for copy in copies:
        copy.wait()


def unpack_own(half, temporal, start, own, after, piece):
    rows, width = start.shape
    n = own.shape[0]
    return pl.pallas_call(
        functools.partial(own_kernel, piece),
        in_specs=[SMEM, VMEM, VMEM, HBM, ANY],
        out_specs=VMEM,
        out_shape=jax.ShapeDtypeStruct((rows, width), F32),
        scratch_shapes=[
            pltpu.VMEM((n * piece, width), BF16),
            pltpu.SemaphoreType.DMA((1, n)),
        ],
        compiler_params=params(50),
        name="unpack_own",
    )(half, temporal, start, own, after)


def unpack_other(half, temporal, start, own, crossed, other, piece, held):
    rows, width = start.shape
    n = own.shape[0]
    weight = pltpu.VMEM((HALVES * n * held, width), BF16)
    return pl.pallas_call(
        functools.partial(other_kernel, piece, held, crossed.shape[1]),
        in_specs=[SMEM, VMEM, VMEM, HBM, HBM, HBM],
        out_specs=[VMEM] * 3,
        out_shape=[pltpu.VMEM((rows, width), F32), weight, weight],
        scratch_shapes=[
            pltpu.VMEM((n * piece, width), BF16),
            pltpu.SemaphoreType.DMA((2, n)),
            pltpu.SemaphoreType.DMA((HALVES, 2, n)),
        ],
        compiler_params=params(44),
        name="unpack_other",
    )(half, temporal, start, own, crossed, other)


def reload_kernel(piece, held, crossed, own_ref, g_ref, after_ref, w1_ref, w2_ref, w_sem):
    copies = [
        copy
        for part, (ref, first) in enumerate(((own_ref, piece), (g_ref, piece - crossed)))
        for copy in weight_copies(ref, first, held, part, w1_ref, w2_ref, w_sem.at[part])
    ]
    for copy in copies:
        copy.start()
    for copy in copies:
        copy.wait()


def reload_weights(own, other, after, crossed, piece, held):
    n, _, width = own.shape
    weight = pltpu.VMEM((HALVES * n * held, width), BF16)
    return pl.pallas_call(
        functools.partial(reload_kernel, piece, held, crossed),
        in_specs=[HBM, HBM, ANY],
        out_specs=[VMEM] * 2,
        out_shape=[weight, weight],
        scratch_shapes=[pltpu.SemaphoreType.DMA((HALVES, 2, n))],
        compiler_params=params(44),
        name="reload_weights",
    )(own, other, after)


def normalise(resid):
    scale = lax.rsqrt(jnp.mean(resid * resid, axis=-1, keepdims=True) + EPS)
    return scale, (resid * scale).astype(BF16)


def received(refs, start):
    for ref in refs:
        start = start + ref[...].astype(F32)
    return start


def forward_kernel(turn_index, code_ref, base_ref, w1_ref, w2_ref, *refs):
    out_ref = refs[-1]

    @pl.when(code_ref[0] == turn_index)
    def _():
        resid = received(refs[:-1], base_ref[...])
        _, normed = normalise(resid)
        pre = dot_nt(normed, w1_ref[...])
        active = (pre * jax.nn.sigmoid(pre)).astype(BF16)
        out_ref[...] = (resid + dot_nn(active, w2_ref[...])).astype(BF16)


def saved_kernel(base_ref, w1_ref, *refs):
    unit_ref, scale_ref, normed_ref, slope_ref, active_ref = refs[-5:]
    resid = received(refs[:-5], base_ref[...])
    scale, normed = normalise(resid)
    unit_ref[...] = resid * scale
    scale_ref[...] = scale
    normed_ref[...] = normed
    pre = dot_nt(normed, w1_ref[...])
    sigma = jax.nn.sigmoid(pre)
    slope_ref[...] = sigma * (1.0 + pre * (1.0 - sigma))
    active_ref[...] = (pre * sigma).astype(BF16).T


def backward_math(state_slope, w1_ref, w2_ref, unit_ref, scale_ref, slope_ref, keep_ref):
    slope_b = state_slope.astype(BF16)
    pre_slope = (dot_nt(slope_b, w2_ref[...]) * slope_ref[...]).astype(BF16)
    if keep_ref is not None:
        keep_ref[...] = pre_slope.T
    norm_slope = dot_nn(pre_slope, w1_ref[...])
    unit = unit_ref[...]
    mean = jnp.mean(norm_slope * unit, axis=-1, keepdims=True)
    carried = state_slope + scale_ref[...] * (norm_slope - unit * mean)
    return carried.astype(BF16), slope_b


def backward_kernel(
    owner, n_got, n_through, code_ref, cot_ref, w1_ref, w2_ref, unit_ref, scale_ref, slope_ref,
    *refs
):
    out_ref = refs[n_got + n_through]

    @pl.when(code_ref[0] == owner)
    def _():
        state_slope = received(refs[:n_got], cot_ref[...])
        out_ref[...], _ = backward_math(
            state_slope, w1_ref, w2_ref, unit_ref, scale_ref, slope_ref, None
        )


def last_kernel(cot_ref, w1_ref, w2_ref, unit_ref, scale_ref, slope_ref, *refs):
    late_ref, pre_ref = refs[-2:]
    width = cot_ref.shape[1]
    state_slope = received(refs[:-2], cot_ref[...])
    late_ref[:, :width], late_ref[:, width:] = backward_math(
        state_slope, w1_ref, w2_ref, unit_ref, scale_ref, slope_ref, pre_ref
    )


def turn(kernel, operands, outs, name, sizes, through=()):
    rows, hidden, width = sizes
    scalar = [SMEM] if operands[0].dtype == jnp.int32 else []
    outs = list(outs)
    count = len(operands)
    return pl.pallas_call(
        kernel,
        in_specs=scalar + [VMEM] * (count - len(scalar)) + [ANY] * len(through),
        out_specs=[VMEM] * len(outs) + [ANY] * len(through),
        out_shape=outs + [jax.ShapeDtypeStruct(array.shape, array.dtype) for array in through],
        input_output_aliases={count + i: len(outs) + i for i in range(len(through))},
        compiler_params=params(10),
        cost_estimate=pl.CostEstimate(
            flops=4 * rows * hidden * width, bytes_accessed=4 * hidden * width, transcendentals=0
        ),
        name=name,
    )(*operands, *through)


def term_kernel(half_ref, c_ref, own_ref, crossed_ref, other_ref, out_ref):
    _, piece, width = own_ref.shape
    own = own_ref[...].reshape(CORES * piece, width)
    parts = [ref[core] for core in range(CORES) for ref in (crossed_ref, other_ref)]
    other = jnp.concatenate(parts, axis=0)
    for part, half in ((own, half_ref[0]), (other, 1 - half_ref[0])):
        out_ref[half] = dot_nt(c_ref[...], part).astype(BF16)


def temporal_terms(half, late, own, crossed, other, n_code, piece):
    rows = late.shape[0]
    n, _, width = own.shape
    total = 2 * n * piece
    first = crossed.shape[1]
    weight = lambda count: pl.BlockSpec((CORES, count, width), lambda x: (x, 0, 0))
    return pl.pallas_call(
        term_kernel,
        grid=(n // CORES,),
        in_specs=[
            SMEM,
            pl.BlockSpec((rows, width), lambda x: (0, 0)),
            weight(piece),
            weight(first),
            weight(piece - first),
        ],
        out_specs=pl.BlockSpec((HALVES, rows, total // n_code), lambda x: (x, 0, 0)),
        out_shape=jax.ShapeDtypeStruct((n_code, rows, total // n_code), BF16),
        compiler_params=params(50),
        cost_estimate=pl.CostEstimate(
            flops=2 * rows * width * total, bytes_accessed=2 * width * total, transcendentals=0
        ),
        name="temporal_terms",
    )(half, late, own, crossed, other)


def grads_kernel(n, final, *refs):
    lefts, g_ref, given, outs = refs[:n], refs[n], refs[n + 1:-n], refs[-n:]
    width = outs[0].shape[1]
    for i in range(n):
        right = g_ref[:, width:] if i == n - 1 else g_ref[:, :width]
        total = dot_nn(lefts[i][...], right)
        if final:
            total = total + given[i][...]
        outs[i][...] = total[: outs[i].shape[0], :].astype(outs[i].dtype)


def row_grads(lefts, gathered, partial, out_rows):
    frames, both = gathered.shape
    width = both // 2
    n = len(lefts)
    final = bool(partial)
    outs = [
        jax.ShapeDtypeStruct((rows, width), BF16 if final else F32)
        for rows in (out_rows if final else [left.shape[0] for left in lefts])
    ]
    operands = (*lefts, gathered, *partial)
    return pl.pallas_call(
        functools.partial(grads_kernel, n, final),
        in_specs=[VMEM] * len(operands),
        out_specs=[VMEM] * n,
        out_shape=outs,
        compiler_params=params(16),
        cost_estimate=pl.CostEstimate(
            flops=2 * sum(left.shape[0] for left in lefts) * width * frames,
            bytes_accessed=2 * frames * both,
            transcendentals=0,
        ),
        name="row_grads",
    )(*operands)


def own_and_other(array, half):
    split = array.reshape((-1, HALVES, CORES) + array.shape[1:])
    pick = lambda which: lax.dynamic_index_in_dim(split, which, 1, keepdims=False)
    return tuple(
        part.reshape((-1,) + array.shape[1:]) for part in (pick(half), pick(1 - half))
    )


def in_dp_order(both, half):
    own, other = (part.reshape((-1, 1, CORES) + part.shape[1:]) for part in both)
    ordered = jnp.where(
        half == 0,
        jnp.concatenate([own, other], axis=1),
        jnp.concatenate([other, own], axis=1),
    )
    return ordered.reshape((-1,) + ordered.shape[3:])


def swap_halves(block, n_dp):
    return lax.ppermute(block, "dp", [(i, i ^ CORES) for i in range(n_dp)])


def gather_half(block, n_dp):
    groups = [
        [i for i in range(n_dp) if i // CORES % HALVES == half] for half in range(HALVES)
    ]
    return lax.all_gather(block, "dp", axis=0, axis_index_groups=groups)


def lanes(pieces):
    return pieces.transpose(1, 0, 2).reshape(pieces.shape[1], -1)


def per_device(
    temporal_out, depth_in, embed, depth_w1, depth_w2, audio_tokens, barge_mask, out_grad
):
    dp_index = lax.axis_index("dp")
    n_dp, n_code = lax.axis_size("dp"), lax.axis_size("code")
    rows = temporal_out.shape[0]
    piece, width = depth_in.shape[1:]
    own_hidden = depth_w1.shape[2]
    table = embed[0]

    pad_hidden = -own_hidden % SUBLANES
    held = own_hidden + pad_hidden
    hidden = held * n_dp
    pad = ((0, pad_hidden), (0, 0))
    shard = jnp.concatenate(
        [depth_in[0], jnp.pad(depth_w1[0].T, pad), jnp.pad(depth_w2[0].T, pad)], axis=0
    )
    half = (dp_index // CORES % HALVES).astype(jnp.int32)
    halves = (half.reshape(1), 1 - half.reshape(1))
    crossing = CROSSING if piece > CROSSING else piece // 2
    own_shards = gather_half(shard, n_dp)
    other_shards = gather_half(swap_halves(shard[crossing:], n_dp), n_dp)
    crossed = swap_halves(own_shards[:, :crossing], n_dp)

    token_all = audio_tokens[:, 0]
    token_own = lax.dynamic_slice_in_dim(token_all, dp_index * rows, rows, 0)
    token_rows = jnp.take(table, token_own, axis=0)
    temporal_pieces = temporal_out.T.reshape(n_dp, piece, rows)
    base = unpack_own(
        halves[0], temporal_out, token_rows, own_shards, temporal_pieces, piece
    )
    base, w_first, w_second = unpack_other(
        halves[1], temporal_out, base, own_shards, crossed, other_shards, piece, held
    )

    code_index = lax.axis_index("code")
    code = code_index.astype(jnp.int32).reshape(1)
    upper = code_index >= n_code // 2
    sizes = (rows, hidden, width)
    state_type = jax.ShapeDtypeStruct((rows, width), BF16)
    got = []
    for step in range(n_code - 1):
        (state,) = turn(
            functools.partial(forward_kernel, step),
            (code, base, w_first, w_second, *got[-1:]),
            [state_type], "forward_turn", sizes,
        )
        got.append(hop(state, "code", step, step + 1))
    unit, scale, normed, slope, active = turn(
        saved_kernel,
        (base, w_first, *got),
        [
            jax.ShapeDtypeStruct((rows, width), F32),
            jax.ShapeDtypeStruct((rows, 1), F32),
            state_type,
            jax.ShapeDtypeStruct((rows, hidden), F32),
            jax.ShapeDtypeStruct((hidden, rows), BF16),
        ],
        "saved_values", sizes,
    )
    by_part = (HALVES, n_dp // HALVES, held, rows)

    def exchanged(_, temporal, active):
        pieces = in_dp_order(active.reshape(by_part), half)
        return lax.all_to_all(jnp.concatenate([temporal, pieces], axis=1), "dp", 0, 0)

    cotangent = out_grad[:, 0, :].astype(F32) * barge_mask.astype(F32)[:, None]
    got = []
    for owner in range(n_code - 1, 0, -1):
        through = () if got else (normed, active)
        saved = (cotangent, w_first, w_second, unit, scale, slope)
        carried, *passed = turn(
            functools.partial(backward_kernel, owner, len(got[-1:]), len(through)),
            (code, *saved, *got[-1:]),
            [state_type], "backward_turn", sizes, through,
        )
        if passed:
            normed, active = passed
            normed_all = lax.all_gather(normed, "dp", axis=0, tiled=True)
            early = jnp.zeros((n_dp, piece + held, rows), BF16)
            early = lax.cond(
                upper, lambda given, *_: given, exchanged, early, temporal_pieces, active
            )
            w_first, w_second = reload_weights(
                own_shards, other_shards, early, crossing, piece, held
            )
        got.append(hop(carried, "code", owner, owner - 1))
    saved = (cotangent, w_first, w_second, unit, scale, slope)
    late, pre_slope = turn(
        last_kernel, (*saved, *got),
        [
            jax.ShapeDtypeStruct((rows, 2 * width), BF16),
            jax.ShapeDtypeStruct((hidden, rows), BF16),
        ],
        "last_values", sizes,
    )

    late_all = (gather_half(late, n_dp), gather_half(swap_halves(late, n_dp), n_dp))
    early = lax.cond(
        upper, exchanged, lambda given, *_: given, early, temporal_pieces, active
    )
    temporal_all, active_all = early[:, :piece], early[:, piece:]
    pre_all = lax.all_to_all(in_dp_order(pre_slope.reshape(by_part), half), "dp", 0, 0)
    terms = temporal_terms(
        halves[0], late, own_shards, crossed, other_shards, n_code, piece
    )
    terms, pre_all = lax.optimization_barrier((terms, pre_all))
    terms = lax.all_to_all(terms, "code", 0, 0)
    temporal_grad = jnp.sum(terms.astype(F32), axis=0).astype(BF16)
    first_grad = dot_nn(lanes(pre_all), normed_all).astype(BF16)

    own_vocab = table.shape[0] // n_dp
    vocab_ids = dp_index * own_vocab + lax.broadcasted_iota(jnp.int32, (own_vocab, 1), 0)
    temporal_parts = own_and_other(temporal_all, half)
    token_parts = own_and_other(token_all.reshape(n_dp, rows), half)
    active_parts = own_and_other(active_all, half)
    grads = ()
    for part in range(HALVES):
        onehot = (token_parts[part].reshape(1, -1) == vocab_ids).astype(BF16)
        grads = row_grads(
            (lanes(temporal_parts[part]), onehot, lanes(active_parts[part])),
            late_all[part].reshape(-1, 2 * width),
            grads,
            (piece, own_vocab, own_hidden),
        )
    in_grad, table_grad, second_grad = grads
    return (
        temporal_grad,
        in_grad[None],
        table_grad[None],
        first_grad[:own_hidden].T[None],
        second_grad.T[None],
    )


def solution(mesh):
    in_specs = (
        P("dp", None),
        P("code", "dp", None),
        P("code", None, None),
        P("code", None, "dp"),
        P("code", None, "dp"),
        P(None, "code"),
        P("dp"),
        P("dp", "code", None),
    )
    out_specs = (
        P("dp", "code"),
        P("code", "dp", None),
        P("code", "dp", None),
        P("code", None, "dp"),
        P("code", None, "dp"),
    )
    return jax.shard_map(
        per_device, mesh=mesh, in_specs=in_specs, out_specs=out_specs, check_vma=False
    )
```

```python
import functools

import jax
import jax.numpy as jnp
from jax import lax
from jax.experimental import pallas as pl
from jax.experimental.pallas import tpu as pltpu
from jax.sharding import PartitionSpec as P

EPS = 1e-06
F32 = jnp.float32
BF16 = jnp.bfloat16
SUBLANES = 8


def dot_nn(left, right):
    return lax.dot_general(left, right, (((1,), (0,)), ((), ())), preferred_element_type=F32)


def dot_nt(left, right):
    return lax.dot_general(left, right, (((1,), (1,)), ((), ())), preferred_element_type=F32)


def hop(block, axis, source, target):
    return lax.ppermute(block, axis, [(source, target)])


VMEM = pl.BlockSpec(memory_space=pltpu.VMEM)
ANY = pl.BlockSpec(memory_space=pl.ANY)
SMEM = pl.BlockSpec(memory_space=pltpu.SMEM)
HBM = pl.BlockSpec(memory_space=pltpu.HBM)
HALVES, CORES = 2, 2
CROSSING = 96


def params(megabytes):
    return pltpu.CompilerParams(vmem_limit_bytes=megabytes * 1024 * 1024)


def add_depth(piece, half_ref, t_ref, start, sources, d_ref, d_sem):
    n = sources[0][0].shape[0]
    span = CORES * piece

    def copies(s):
        first = 0
        for i, (ref, count) in enumerate(sources):
            yield pltpu.make_async_copy(
                ref.at[s, pl.ds(0, count)],
                d_ref.at[pl.ds(s * piece + first, count)],
                d_sem.at[i, s],
            )
            first += count

    for s in range(n):
        for copy in copies(s):
            copy.start()

    def total():
        result = start
        for x in range(n // CORES):
            for core in range(CORES):
                for copy in copies(x * CORES + core):
                    copy.wait()
            column = pl.multiple_of((x * HALVES + half_ref[0]) * span, span)
            part = d_ref[pl.ds(x * span, span), :]
            result = result + dot_nn(t_ref[:, pl.ds(column, span)], part)
        return result

    return total


def weight_copies(ref, first, held, part, w1_ref, w2_ref, w_sem):
    n = ref.shape[0]
    return [
        pltpu.make_async_copy(
            ref.at[s, pl.ds(first + which * held, held)],
            to_ref.at[pl.ds((part * n + s) * held, held)],
            w_sem.at[which, s],
        )
        for which, to_ref in enumerate((w1_ref, w2_ref))
        for s in range(n)
    ]


def own_kernel(piece, half_ref, t_ref, start_ref, g_ref, after_ref, base_ref, d_ref, d_sem):
    start = start_ref[...].astype(F32)
    sources = ((g_ref, piece),)
    base_ref[...] = add_depth(piece, half_ref, t_ref, start, sources, d_ref, d_sem)()


def other_kernel(piece, held, crossed, half_ref, t_ref, start_ref, own_ref, r_ref, g_ref,
                 base_ref, w1_ref, w2_ref, d_ref, d_sem, w_sem):
    rest = piece - crossed
    sources = ((r_ref, crossed), (g_ref, rest))
    total = add_depth(piece, half_ref, t_ref, start_ref[...], sources, d_ref, d_sem)
    copies = [
        copy
        for part, (ref, first) in enumerate(((own_ref, piece), (g_ref, rest)))
        for copy in weight_copies(ref, first, held, part, w1_ref, w2_ref, w_sem.at[part])
    ]
    for copy in copies:
        copy.start()
    base_ref[...] = total()
    for copy in copies:
        copy.wait()


def unpack_own(half, temporal, start, own, after, piece):
    rows, width = start.shape
    n = own.shape[0]
    return pl.pallas_call(
        functools.partial(own_kernel, piece),
        in_specs=[SMEM, VMEM, VMEM, HBM, ANY],
        out_specs=VMEM,
        out_shape=jax.ShapeDtypeStruct((rows, width), F32),
        scratch_shapes=[
            pltpu.VMEM((n * piece, width), BF16),
            pltpu.SemaphoreType.DMA((1, n)),
        ],
        compiler_params=params(50),
        name="unpack_own",
    )(half, temporal, start, own, after)


def unpack_other(half, temporal, start, own, crossed, other, piece, held):
    rows, width = start.shape
    n = own.shape[0]
    weight = pltpu.VMEM((HALVES * n * held, width), BF16)
    return pl.pallas_call(
        functools.partial(other_kernel, piece, held, crossed.shape[1]),
        in_specs=[SMEM, VMEM, VMEM, HBM, HBM, HBM],
        out_specs=[VMEM] * 3,
        out_shape=[pltpu.VMEM((rows, width), F32), weight, weight],
        scratch_shapes=[
            pltpu.VMEM((n * piece, width), BF16),
            pltpu.SemaphoreType.DMA((2, n)),
            pltpu.SemaphoreType.DMA((HALVES, 2, n)),
        ],
        compiler_params=params(44),
        name="unpack_other",
    )(half, temporal, start, own, crossed, other)


def reload_kernel(piece, held, crossed, own_ref, g_ref, after_ref, w1_ref, w2_ref, w_sem):
    copies = [
        copy
        for part, (ref, first) in enumerate(((own_ref, piece), (g_ref, piece - crossed)))
        for copy in weight_copies(ref, first, held, part, w1_ref, w2_ref, w_sem.at[part])
    ]
    for copy in copies:
        copy.start()
    for copy in copies:
        copy.wait()


def reload_weights(own, other, after, crossed, piece, held):
    n, _, width = own.shape
    weight = pltpu.VMEM((HALVES * n * held, width), BF16)
    return pl.pallas_call(
        functools.partial(reload_kernel, piece, held, crossed),
        in_specs=[HBM, HBM, ANY],
        out_specs=[VMEM] * 2,
        out_shape=[weight, weight],
        scratch_shapes=[pltpu.SemaphoreType.DMA((HALVES, 2, n))],
        compiler_params=params(44),
        name="reload_weights",
    )(own, other, after)


def normalise(resid):
    scale = lax.rsqrt(jnp.mean(resid * resid, axis=-1, keepdims=True) + EPS)
    return scale, (resid * scale).astype(BF16)


def received(refs, start):
    for ref in refs:
        start = start + ref[...].astype(F32)
    return start


def forward_kernel(turn_index, code_ref, base_ref, w1_ref, w2_ref, *refs):
    out_ref = refs[-1]

    @pl.when(code_ref[0] == turn_index)
    def _():
        resid = received(refs[:-1], base_ref[...])
        _, normed = normalise(resid)
        pre = dot_nt(normed, w1_ref[...])
        active = (pre * jax.nn.sigmoid(pre)).astype(BF16)
        out_ref[...] = (resid + dot_nn(active, w2_ref[...])).astype(BF16)


def saved_kernel(base_ref, w1_ref, *refs):
    unit_ref, scale_ref, normed_ref, slope_ref, active_ref = refs[-5:]
    resid = received(refs[:-5], base_ref[...])
    scale, normed = normalise(resid)
    unit_ref[...] = resid * scale
    scale_ref[...] = scale
    normed_ref[...] = normed
    pre = dot_nt(normed, w1_ref[...])
    sigma = jax.nn.sigmoid(pre)
    slope_ref[...] = sigma * (1.0 + pre * (1.0 - sigma))
    active_ref[...] = (pre * sigma).astype(BF16).T


def backward_math(state_slope, w1_ref, w2_ref, unit_ref, scale_ref, slope_ref, keep_ref):
    slope_b = state_slope.astype(BF16)
    pre_slope = (dot_nt(slope_b, w2_ref[...]) * slope_ref[...]).astype(BF16)
    if keep_ref is not None:
        keep_ref[...] = pre_slope.T
    norm_slope = dot_nn(pre_slope, w1_ref[...])
    unit = unit_ref[...]
    mean = jnp.mean(norm_slope * unit, axis=-1, keepdims=True)
    carried = state_slope + scale_ref[...] * (norm_slope - unit * mean)
    return carried.astype(BF16), slope_b


def backward_kernel(
    owner, n_got, n_through, code_ref, cot_ref, w1_ref, w2_ref, unit_ref, scale_ref, slope_ref,
    *refs
):
    out_ref = refs[n_got + n_through]

    @pl.when(code_ref[0] == owner)
    def _():
        state_slope = received(refs[:n_got], cot_ref[...])
        out_ref[...], _ = backward_math(
            state_slope, w1_ref, w2_ref, unit_ref, scale_ref, slope_ref, None
        )


def last_kernel(cot_ref, w1_ref, w2_ref, unit_ref, scale_ref, slope_ref, *refs):
    late_ref, pre_ref = refs[-2:]
    width = cot_ref.shape[1]
    state_slope = received(refs[:-2], cot_ref[...])
    late_ref[:, :width], late_ref[:, width:] = backward_math(
        state_slope, w1_ref, w2_ref, unit_ref, scale_ref, slope_ref, pre_ref
    )


def turn(kernel, operands, outs, name, sizes, through=()):
    rows, hidden, width = sizes
    scalar = [SMEM] if operands[0].dtype == jnp.int32 else []
    outs = list(outs)
    count = len(operands)
    return pl.pallas_call(
        kernel,
        in_specs=scalar + [VMEM] * (count - len(scalar)) + [ANY] * len(through),
        out_specs=[VMEM] * len(outs) + [ANY] * len(through),
        out_shape=outs + [jax.ShapeDtypeStruct(array.shape, array.dtype) for array in through],
        input_output_aliases={count + i: len(outs) + i for i in range(len(through))},
        compiler_params=params(10),
        cost_estimate=pl.CostEstimate(
            flops=4 * rows * hidden * width, bytes_accessed=4 * hidden * width, transcendentals=0
        ),
        name=name,
    )(*operands, *through)


def term_kernel(half_ref, c_ref, own_ref, crossed_ref, other_ref, out_ref):
    _, piece, width = own_ref.shape
    own = own_ref[...].reshape(CORES * piece, width)
    parts = [ref[core] for core in range(CORES) for ref in (crossed_ref, other_ref)]
    other = jnp.concatenate(parts, axis=0)
    for part, half in ((own, half_ref[0]), (other, 1 - half_ref[0])):
        out_ref[half] = dot_nt(c_ref[...], part).astype(BF16)


def temporal_terms(half, late, own, crossed, other, n_code, piece):
    rows = late.shape[0]
    n, _, width = own.shape
    total = 2 * n * piece
    first = crossed.shape[1]
    weight = lambda count: pl.BlockSpec((CORES, count, width), lambda x: (x, 0, 0))
    return pl.pallas_call(
        term_kernel,
        grid=(n // CORES,),
        in_specs=[
            SMEM,
            pl.BlockSpec((rows, width), lambda x: (0, 0)),
            weight(piece),
            weight(first),
            weight(piece - first),
        ],
        out_specs=pl.BlockSpec((HALVES, rows, total // n_code), lambda x: (x, 0, 0)),
        out_shape=jax.ShapeDtypeStruct((n_code, rows, total // n_code), BF16),
        compiler_params=params(50),
        cost_estimate=pl.CostEstimate(
            flops=2 * rows * width * total, bytes_accessed=2 * width * total, transcendentals=0
        ),
        name="temporal_terms",
    )(half, late, own, crossed, other)


def grads_kernel(n, blocks, *refs):
    final = len(refs) == 2 * (2 * n + 1) + n + 2
    count = 2 * n + 1 if final else n + 1
    ins, refs = refs[:count], refs[count:]
    outs, refs = refs[:n], refs[n:]
    bufs, g_sem, in_sem = refs[:count], refs[-2], refs[-1]
    width = outs[0].shape[1]
    block = ins[n].shape[0] // blocks
    rows = [pl.ds(i * block, block) for i in range(blocks)]
    loads = [
        pltpu.make_async_copy(ins[n].at[part], bufs[n].at[part], g_sem.at[i])
        for i, part in enumerate(rows)
    ]
    others = [
        pltpu.make_async_copy(ins[i], bufs[i], in_sem.at[i]) for i in range(count) if i != n
    ]
    for copy in others[:n] + loads + others[n:]:
        copy.start()
    for copy in others[:n]:
        copy.wait()
    totals = [None] * n
    for load, part in zip(loads, rows):
        load.wait()
        for i in range(n):
            columns = pl.ds(width, width) if i == n - 1 else pl.ds(0, width)
            product = dot_nn(bufs[i][:, part], bufs[n][part, columns])
            totals[i] = product if totals[i] is None else totals[i] + product
    for copy in others[n:]:
        copy.wait()
    for i in range(n):
        total = totals[i] + bufs[n + 1 + i][...] if final else totals[i]
        outs[i][...] = total[: outs[i].shape[0], :].astype(outs[i].dtype)


def row_grads(lefts, gathered, partial, out_rows):
    frames, both = gathered.shape
    width = both // 2
    n = len(lefts)
    final = bool(partial)
    blocks = 2 if frames % 512 == 0 else 1
    outs = [
        jax.ShapeDtypeStruct((rows, width), BF16 if final else F32)
        for rows in (out_rows if final else [left.shape[0] for left in lefts])
    ]
    operands = (*lefts, gathered, *partial)
    return pl.pallas_call(
        functools.partial(grads_kernel, n, blocks),
        in_specs=[HBM] * len(operands),
        out_specs=[VMEM] * n,
        out_shape=outs,
        scratch_shapes=[pltpu.VMEM(array.shape, array.dtype) for array in operands]
        + [pltpu.SemaphoreType.DMA((blocks,)), pltpu.SemaphoreType.DMA((len(operands),))],
        compiler_params=params(58),
        cost_estimate=pl.CostEstimate(
            flops=2 * sum(left.shape[0] for left in lefts) * width * frames,
            bytes_accessed=2 * frames * both,
            transcendentals=0,
        ),
        name="row_grads",
    )(*operands)


def own_and_other(array, half):
    split = array.reshape((-1, HALVES, CORES) + array.shape[1:])
    pick = lambda which: lax.dynamic_index_in_dim(split, which, 1, keepdims=False)
    return tuple(
        part.reshape((-1,) + array.shape[1:]) for part in (pick(half), pick(1 - half))
    )


def in_dp_order(both, half):
    own, other = (part.reshape((-1, 1, CORES) + part.shape[1:]) for part in both)
    ordered = jnp.where(
        half == 0,
        jnp.concatenate([own, other], axis=1),
        jnp.concatenate([other, own], axis=1),
    )
    return ordered.reshape((-1,) + ordered.shape[3:])


def swap_halves(block, n_dp):
    return lax.ppermute(block, "dp", [(i, i ^ CORES) for i in range(n_dp)])


def gather_half(block, n_dp):
    groups = [
        [i for i in range(n_dp) if i // CORES % HALVES == half] for half in range(HALVES)
    ]
    return lax.all_gather(block, "dp", axis=0, axis_index_groups=groups)


def lanes(pieces):
    return pieces.transpose(1, 0, 2).reshape(pieces.shape[1], -1)


def per_device(
    temporal_out, depth_in, embed, depth_w1, depth_w2, audio_tokens, barge_mask, out_grad
):
    dp_index = lax.axis_index("dp")
    n_dp, n_code = lax.axis_size("dp"), lax.axis_size("code")
    rows = temporal_out.shape[0]
    piece, width = depth_in.shape[1:]
    own_hidden = depth_w1.shape[2]
    table = embed[0]

    pad_hidden = -own_hidden % SUBLANES
    held = own_hidden + pad_hidden
    hidden = held * n_dp
    pad = ((0, pad_hidden), (0, 0))
    shard = jnp.concatenate(
        [depth_in[0], jnp.pad(depth_w1[0].T, pad), jnp.pad(depth_w2[0].T, pad)], axis=0
    )
    half = (dp_index // CORES % HALVES).astype(jnp.int32)
    halves = (half.reshape(1), 1 - half.reshape(1))
    crossing = CROSSING if piece > CROSSING else piece // 2
    own_shards = gather_half(shard, n_dp)
    other_shards = gather_half(swap_halves(shard[crossing:], n_dp), n_dp)
    crossed = swap_halves(own_shards[:, :crossing], n_dp)

    token_all = audio_tokens[:, 0]
    token_own = lax.dynamic_slice_in_dim(token_all, dp_index * rows, rows, 0)
    token_rows = jnp.take(table, token_own, axis=0)
    temporal_pieces = temporal_out.T.reshape(n_dp, piece, rows)
    base = unpack_own(
        halves[0], temporal_out, token_rows, own_shards, temporal_pieces, piece
    )
    base, w_first, w_second = unpack_other(
        halves[1], temporal_out, base, own_shards, crossed, other_shards, piece, held
    )

    code_index = lax.axis_index("code")
    code = code_index.astype(jnp.int32).reshape(1)
    upper = code_index >= n_code // 2
    sizes = (rows, hidden, width)
    state_type = jax.ShapeDtypeStruct((rows, width), BF16)
    got = []
    for step in range(n_code - 1):
        (state,) = turn(
            functools.partial(forward_kernel, step),
            (code, base, w_first, w_second, *got[-1:]),
            [state_type], "forward_turn", sizes,
        )
        got.append(hop(state, "code", step, step + 1))
    unit, scale, normed, slope, active = turn(
        saved_kernel,
        (base, w_first, *got),
        [
            jax.ShapeDtypeStruct((rows, width), F32),
            jax.ShapeDtypeStruct((rows, 1), F32),
            state_type,
            jax.ShapeDtypeStruct((rows, hidden), F32),
            jax.ShapeDtypeStruct((hidden, rows), BF16),
        ],
        "saved_values", sizes,
    )
    by_part = (HALVES, n_dp // HALVES, held, rows)

    def exchanged(_, temporal, active):
        pieces = in_dp_order(active.reshape(by_part), half)
        return lax.all_to_all(jnp.concatenate([temporal, pieces], axis=1), "dp", 0, 0)

    cotangent = out_grad[:, 0, :].astype(F32) * barge_mask.astype(F32)[:, None]
    got = []
    for owner in range(n_code - 1, 0, -1):
        through = () if got else (normed, active)
        saved = (cotangent, w_first, w_second, unit, scale, slope)
        carried, *passed = turn(
            functools.partial(backward_kernel, owner, len(got[-1:]), len(through)),
            (code, *saved, *got[-1:]),
            [state_type], "backward_turn", sizes, through,
        )
        if passed:
            normed, active = passed
            normed_all = lax.all_gather(normed, "dp", axis=0, tiled=True)
            early = jnp.zeros((n_dp, piece + held, rows), BF16)
            early = lax.cond(
                upper, lambda given, *_: given, exchanged, early, temporal_pieces, active
            )
            w_first, w_second = reload_weights(
                own_shards, other_shards, early, crossing, piece, held
            )
        got.append(hop(carried, "code", owner, owner - 1))
    saved = (cotangent, w_first, w_second, unit, scale, slope)
    late, pre_slope = turn(
        last_kernel, (*saved, *got),
        [
            jax.ShapeDtypeStruct((rows, 2 * width), BF16),
            jax.ShapeDtypeStruct((hidden, rows), BF16),
        ],
        "last_values", sizes,
    )

    early = lax.cond(
        upper, exchanged, lambda given, *_: given, early, temporal_pieces, active
    )
    own_late = gather_half(late, n_dp)
    late_rows, early = lax.optimization_barrier((late, early))
    late_all = (own_late, gather_half(swap_halves(late_rows, n_dp), n_dp))
    temporal_all, active_all = early[:, :piece], early[:, piece:]
    pre_all = lax.all_to_all(in_dp_order(pre_slope.reshape(by_part), half), "dp", 0, 0)
    terms = temporal_terms(
        halves[0], late, own_shards, crossed, other_shards, n_code, piece
    )
    terms, pre_all = lax.optimization_barrier((terms, pre_all))
    terms = lax.all_to_all(terms, "code", 0, 0)
    temporal_grad = jnp.sum(terms.astype(F32), axis=0).astype(BF16)
    first_grad = dot_nn(lanes(pre_all), normed_all).astype(BF16)

    own_vocab = table.shape[0] // n_dp
    vocab_ids = dp_index * own_vocab + lax.broadcasted_iota(jnp.int32, (own_vocab, 1), 0)
    temporal_parts = own_and_other(temporal_all, half)
    token_parts = own_and_other(token_all.reshape(n_dp, rows), half)
    active_parts = own_and_other(active_all, half)
    grads = ()
    for part in range(HALVES):
        onehot = (token_parts[part].reshape(1, -1) == vocab_ids).astype(BF16)
        grads = row_grads(
            (lanes(temporal_parts[part]), onehot, lanes(active_parts[part])),
            late_all[part].reshape(-1, 2 * width),
            grads,
            (piece, own_vocab, own_hidden),
        )
    in_grad, table_grad, second_grad = grads
    return (
        temporal_grad,
        in_grad[None],
        table_grad[None],
        first_grad[:own_hidden].T[None],
        second_grad.T[None],
    )


def solution(mesh):
    in_specs = (
        P("dp", None),
        P("code", "dp", None),
        P("code", None, None),
        P("code", None, "dp"),
        P("code", None, "dp"),
        P(None, "code"),
        P("dp"),
        P("dp", "code", None),
    )
    out_specs = (
        P("dp", "code"),
        P("code", "dp", None),
        P("code", "dp", None),
        P("code", None, "dp"),
        P("code", None, "dp"),
    )
    return jax.shard_map(
        per_device, mesh=mesh, in_specs=in_specs, out_specs=out_specs, check_vma=False
    )
```

```python
import functools

import jax
import jax.numpy as jnp
from jax import lax
from jax.experimental import pallas as pl
from jax.experimental.pallas import tpu as pltpu
from jax.sharding import PartitionSpec as P

EPS = 1e-06
F32 = jnp.float32
BF16 = jnp.bfloat16
SUBLANES = 8


def dot_nn(left, right):
    return lax.dot_general(left, right, (((1,), (0,)), ((), ())), preferred_element_type=F32)


def dot_nt(left, right):
    return lax.dot_general(left, right, (((1,), (1,)), ((), ())), preferred_element_type=F32)


def hop(block, axis, source, target):
    return lax.ppermute(block, axis, [(source, target)])


VMEM = pl.BlockSpec(memory_space=pltpu.VMEM)
ANY = pl.BlockSpec(memory_space=pl.ANY)
SMEM = pl.BlockSpec(memory_space=pltpu.SMEM)
HBM = pl.BlockSpec(memory_space=pltpu.HBM)
HALVES, CORES = 2, 2
CROSSING = 96


def params(megabytes):
    return pltpu.CompilerParams(vmem_limit_bytes=megabytes * 1024 * 1024)


def add_depth(piece, half_ref, t_ref, start, sources, d_ref, d_sem):
    n = sources[0][0].shape[0]
    span = CORES * piece

    def copies(s):
        first = 0
        for i, (ref, count) in enumerate(sources):
            yield pltpu.make_async_copy(
                ref.at[s, pl.ds(0, count)],
                d_ref.at[pl.ds(s * piece + first, count)],
                d_sem.at[i, s],
            )
            first += count

    for s in range(n):
        for copy in copies(s):
            copy.start()

    def total():
        result = start
        for x in range(n // CORES):
            for core in range(CORES):
                for copy in copies(x * CORES + core):
                    copy.wait()
            column = pl.multiple_of((x * HALVES + half_ref[0]) * span, span)
            part = d_ref[pl.ds(x * span, span), :]
            result = result + dot_nn(t_ref[:, pl.ds(column, span)], part)
        return result

    return total


def weight_copies(ref, first, held, part, w1_ref, w2_ref, w_sem):
    n = ref.shape[0]
    return [
        pltpu.make_async_copy(
            ref.at[s, pl.ds(first + which * held, held)],
            to_ref.at[pl.ds((part * n + s) * held, held)],
            w_sem.at[which, s],
        )
        for which, to_ref in enumerate((w1_ref, w2_ref))
        for s in range(n)
    ]


def own_kernel(piece, half_ref, t_ref, start_ref, g_ref, after_ref, base_ref, d_ref, d_sem):
    start = start_ref[...].astype(F32)
    sources = ((g_ref, piece),)
    base_ref[...] = add_depth(piece, half_ref, t_ref, start, sources, d_ref, d_sem)()


def other_kernel(piece, held, crossed, half_ref, t_ref, start_ref, own_ref, r_ref, g_ref,
                 base_ref, w1_ref, w2_ref, d_ref, d_sem, w_sem):
    rest = piece - crossed
    sources = ((r_ref, crossed), (g_ref, rest))
    total = add_depth(piece, half_ref, t_ref, start_ref[...], sources, d_ref, d_sem)
    copies = [
        copy
        for part, (ref, first) in enumerate(((own_ref, piece), (g_ref, rest)))
        for copy in weight_copies(ref, first, held, part, w1_ref, w2_ref, w_sem.at[part])
    ]
    for copy in copies:
        copy.start()
    base_ref[...] = total()
    for copy in copies:
        copy.wait()


def unpack_own(half, temporal, start, own, after, piece):
    rows, width = start.shape
    n = own.shape[0]
    return pl.pallas_call(
        functools.partial(own_kernel, piece),
        in_specs=[SMEM, VMEM, VMEM, HBM, ANY],
        out_specs=VMEM,
        out_shape=jax.ShapeDtypeStruct((rows, width), F32),
        scratch_shapes=[
            pltpu.VMEM((n * piece, width), BF16),
            pltpu.SemaphoreType.DMA((1, n)),
        ],
        compiler_params=params(50),
        name="unpack_own",
    )(half, temporal, start, own, after)


def unpack_other(half, temporal, start, own, crossed, other, piece, held):
    rows, width = start.shape
    n = own.shape[0]
    weight = pltpu.VMEM((HALVES * n * held, width), BF16)
    return pl.pallas_call(
        functools.partial(other_kernel, piece, held, crossed.shape[1]),
        in_specs=[SMEM, VMEM, VMEM, HBM, HBM, HBM],
        out_specs=[VMEM] * 3,
        out_shape=[pltpu.VMEM((rows, width), F32), weight, weight],
        scratch_shapes=[
            pltpu.VMEM((n * piece, width), BF16),
            pltpu.SemaphoreType.DMA((2, n)),
            pltpu.SemaphoreType.DMA((HALVES, 2, n)),
        ],
        compiler_params=params(44),
        name="unpack_other",
    )(half, temporal, start, own, crossed, other)


def reload_kernel(piece, held, crossed, own_ref, g_ref, after_ref, w1_ref, w2_ref, w_sem):
    copies = [
        copy
        for part, (ref, first) in enumerate(((own_ref, piece), (g_ref, piece - crossed)))
        for copy in weight_copies(ref, first, held, part, w1_ref, w2_ref, w_sem.at[part])
    ]
    for copy in copies:
        copy.start()
    for copy in copies:
        copy.wait()


def reload_weights(own, other, after, crossed, piece, held):
    n, _, width = own.shape
    weight = pltpu.VMEM((HALVES * n * held, width), BF16)
    return pl.pallas_call(
        functools.partial(reload_kernel, piece, held, crossed),
        in_specs=[HBM, HBM, ANY],
        out_specs=[VMEM] * 2,
        out_shape=[weight, weight],
        scratch_shapes=[pltpu.SemaphoreType.DMA((HALVES, 2, n))],
        compiler_params=params(44),
        name="reload_weights",
    )(own, other, after)


def normalise(resid):
    scale = lax.rsqrt(jnp.mean(resid * resid, axis=-1, keepdims=True) + EPS)
    return scale, (resid * scale).astype(BF16)


def received(refs, start):
    for ref in refs:
        start = start + ref[...].astype(F32)
    return start


def forward_kernel(turn_index, code_ref, base_ref, w1_ref, w2_ref, *refs):
    out_ref = refs[-1]

    @pl.when(code_ref[0] == turn_index)
    def _():
        resid = received(refs[:-1], base_ref[...])
        _, normed = normalise(resid)
        pre = dot_nt(normed, w1_ref[...])
        active = (pre * jax.nn.sigmoid(pre)).astype(BF16)
        out_ref[...] = (resid + dot_nn(active, w2_ref[...])).astype(BF16)


def saved_kernel(base_ref, w1_ref, *refs):
    unit_ref, scale_ref, normed_ref, slope_ref, active_ref = refs[-5:]
    resid = received(refs[:-5], base_ref[...])
    scale, normed = normalise(resid)
    unit_ref[...] = resid * scale
    scale_ref[...] = scale
    normed_ref[...] = normed
    pre = dot_nt(normed, w1_ref[...])
    sigma = jax.nn.sigmoid(pre)
    slope_ref[...] = sigma * (1.0 + pre * (1.0 - sigma))
    active_ref[...] = (pre * sigma).astype(BF16).T


def backward_math(state_slope, w1_ref, w2_ref, unit_ref, scale_ref, slope_ref, keep_ref):
    slope_b = state_slope.astype(BF16)
    pre_slope = (dot_nt(slope_b, w2_ref[...]) * slope_ref[...]).astype(BF16)
    if keep_ref is not None:
        keep_ref[...] = pre_slope.T
    norm_slope = dot_nn(pre_slope, w1_ref[...])
    unit = unit_ref[...]
    mean = jnp.mean(norm_slope * unit, axis=-1, keepdims=True)
    carried = state_slope + scale_ref[...] * (norm_slope - unit * mean)
    return carried.astype(BF16), slope_b


def backward_kernel(
    owner, n_got, n_through, code_ref, cot_ref, w1_ref, w2_ref, unit_ref, scale_ref, slope_ref,
    *refs
):
    out_ref = refs[n_got + n_through]

    @pl.when(code_ref[0] == owner)
    def _():
        state_slope = received(refs[:n_got], cot_ref[...])
        out_ref[...], _ = backward_math(
            state_slope, w1_ref, w2_ref, unit_ref, scale_ref, slope_ref, None
        )


def last_kernel(cot_ref, w1_ref, w2_ref, unit_ref, scale_ref, slope_ref, *refs):
    late_ref, pre_ref = refs[-2:]
    width = cot_ref.shape[1]
    state_slope = received(refs[:-2], cot_ref[...])
    late_ref[:, :width], late_ref[:, width:] = backward_math(
        state_slope, w1_ref, w2_ref, unit_ref, scale_ref, slope_ref, pre_ref
    )


def turn(kernel, operands, outs, name, sizes, through=()):
    rows, hidden, width = sizes
    scalar = [SMEM] if operands[0].dtype == jnp.int32 else []
    outs = list(outs)
    count = len(operands)
    return pl.pallas_call(
        kernel,
        in_specs=scalar + [VMEM] * (count - len(scalar)) + [ANY] * len(through),
        out_specs=[VMEM] * len(outs) + [ANY] * len(through),
        out_shape=outs + [jax.ShapeDtypeStruct(array.shape, array.dtype) for array in through],
        input_output_aliases={count + i: len(outs) + i for i in range(len(through))},
        compiler_params=params(10),
        cost_estimate=pl.CostEstimate(
            flops=4 * rows * hidden * width, bytes_accessed=4 * hidden * width, transcendentals=0
        ),
        name=name,
    )(*operands, *through)


def term_kernel(half_ref, c_ref, own_ref, crossed_ref, other_ref, out_ref):
    _, piece, width = own_ref.shape
    own = own_ref[...].reshape(CORES * piece, width)
    parts = [ref[core] for core in range(CORES) for ref in (crossed_ref, other_ref)]
    other = jnp.concatenate(parts, axis=0)
    for part, half in ((own, half_ref[0]), (other, 1 - half_ref[0])):
        out_ref[half] = dot_nt(c_ref[...], part).astype(BF16)


def temporal_terms(half, late, own, crossed, other, n_code, piece):
    rows = late.shape[0]
    n, _, width = own.shape
    total = 2 * n * piece
    first = crossed.shape[1]
    weight = lambda count: pl.BlockSpec((CORES, count, width), lambda x: (x, 0, 0))
    return pl.pallas_call(
        term_kernel,
        grid=(n // CORES,),
        in_specs=[
            SMEM,
            pl.BlockSpec((rows, width), lambda x: (0, 0)),
            weight(piece),
            weight(first),
            weight(piece - first),
        ],
        out_specs=pl.BlockSpec((HALVES, rows, total // n_code), lambda x: (x, 0, 0)),
        out_shape=jax.ShapeDtypeStruct((n_code, rows, total // n_code), BF16),
        compiler_params=params(50),
        cost_estimate=pl.CostEstimate(
            flops=2 * rows * width * total, bytes_accessed=2 * width * total, transcendentals=0
        ),
        name="temporal_terms",
    )(half, late, own, crossed, other)


def grads_kernel(blocks, final, *refs):
    n = 3
    count = 2 * n + 1 if final else n + 1
    ins, outs, (first_ref, last_ref, g_ref, *given), (g_sem, in_sem) = (
        refs[:count], refs[count:count + n], refs[count + n:-2], refs[-2:]
    )
    width = outs[0].shape[1]
    block = g_ref.shape[0] // blocks
    rows = [pl.ds(i * block, block) for i in range(blocks)]
    split = ins[0].shape[0]
    targets = [
        first_ref.at[pl.ds(0, split)],
        first_ref.at[pl.ds(split, ins[1].shape[0])],
        last_ref,
        *given,
    ]
    sources = [*ins[:n], *ins[n + 1:]]
    others = [
        pltpu.make_async_copy(source, target, in_sem.at[i])
        for i, (source, target) in enumerate(zip(sources, targets))
    ]
    loads = [
        pltpu.make_async_copy(ins[n].at[part], g_ref.at[part], g_sem.at[i])
        for i, part in enumerate(rows)
    ]
    for copy in others[:n] + loads + others[n:]:
        copy.start()
    for copy in others[:n]:
        copy.wait()
    totals = [None, None]
    for load, part in zip(loads, rows):
        load.wait()
        for i, left_ref in enumerate((first_ref, last_ref)):
            product = dot_nn(left_ref[:, part], g_ref[part, pl.ds(i * width, width)])
            totals[i] = product if totals[i] is None else totals[i] + product
    for copy in others[n:]:
        copy.wait()
    totals = [totals[0][:split], totals[0][split:], totals[1]]
    for i, total in enumerate(totals):
        total = total + given[i][...] if final else total
        outs[i][...] = total[: outs[i].shape[0], :].astype(outs[i].dtype)


def row_grads(lefts, gathered, partial, out_rows):
    frames, both = gathered.shape
    width = both // 2
    final = bool(partial)
    blocks = 2 if frames % 512 == 0 else 1
    outs = [
        jax.ShapeDtypeStruct((rows, width), BF16 if final else F32)
        for rows in (out_rows if final else [left.shape[0] for left in lefts])
    ]
    operands = (*lefts, gathered, *partial)
    first = (lefts[0].shape[0] + lefts[1].shape[0], frames)
    return pl.pallas_call(
        functools.partial(grads_kernel, blocks, final),
        in_specs=[HBM] * len(operands),
        out_specs=[VMEM] * len(outs),
        out_shape=outs,
        scratch_shapes=[
            pltpu.VMEM(first, BF16),
            pltpu.VMEM(lefts[2].shape, BF16),
            pltpu.VMEM(gathered.shape, BF16),
            *[pltpu.VMEM(part.shape, F32) for part in partial],
            pltpu.SemaphoreType.DMA((blocks,)),
            pltpu.SemaphoreType.DMA((len(operands) - 1,)),
        ],
        compiler_params=params(58),
        cost_estimate=pl.CostEstimate(
            flops=2 * sum(left.shape[0] for left in lefts) * width * frames,
            bytes_accessed=2 * frames * both,
            transcendentals=0,
        ),
        name="row_grads",
    )(*operands)


def own_and_other(array, half):
    split = array.reshape((-1, HALVES, CORES) + array.shape[1:])
    pick = lambda which: lax.dynamic_index_in_dim(split, which, 1, keepdims=False)
    return tuple(
        part.reshape((-1,) + array.shape[1:]) for part in (pick(half), pick(1 - half))
    )


def in_dp_order(both, half):
    own, other = (part.reshape((-1, 1, CORES) + part.shape[1:]) for part in both)
    ordered = jnp.where(
        half == 0,
        jnp.concatenate([own, other], axis=1),
        jnp.concatenate([other, own], axis=1),
    )
    return ordered.reshape((-1,) + ordered.shape[3:])


def swap_halves(block, n_dp):
    return lax.ppermute(block, "dp", [(i, i ^ CORES) for i in range(n_dp)])


def gather_half(block, n_dp):
    groups = [
        [i for i in range(n_dp) if i // CORES % HALVES == half] for half in range(HALVES)
    ]
    return lax.all_gather(block, "dp", axis=0, axis_index_groups=groups)


def lanes(pieces):
    return pieces.transpose(1, 0, 2).reshape(pieces.shape[1], -1)


def per_device(
    temporal_out, depth_in, embed, depth_w1, depth_w2, audio_tokens, barge_mask, out_grad
):
    dp_index = lax.axis_index("dp")
    n_dp, n_code = lax.axis_size("dp"), lax.axis_size("code")
    rows = temporal_out.shape[0]
    piece, width = depth_in.shape[1:]
    own_hidden = depth_w1.shape[2]
    table = embed[0]

    pad_hidden = -own_hidden % SUBLANES
    held = own_hidden + pad_hidden
    hidden = held * n_dp
    pad = ((0, pad_hidden), (0, 0))
    shard = jnp.concatenate(
        [depth_in[0], jnp.pad(depth_w1[0].T, pad), jnp.pad(depth_w2[0].T, pad)], axis=0
    )
    half = (dp_index // CORES % HALVES).astype(jnp.int32)
    halves = (half.reshape(1), 1 - half.reshape(1))
    crossing = CROSSING if piece > CROSSING else piece // 2
    own_shards = gather_half(shard, n_dp)
    other_shards = gather_half(swap_halves(shard[crossing:], n_dp), n_dp)
    crossed = swap_halves(own_shards[:, :crossing], n_dp)

    token_all = audio_tokens[:, 0]
    token_own = lax.dynamic_slice_in_dim(token_all, dp_index * rows, rows, 0)
    token_rows = jnp.take(table, token_own, axis=0)
    code_index = lax.axis_index("code")
    upper = code_index >= n_code // 2
    temporal_pieces = lax.cond(
        upper,
        lambda pieces: lax.all_to_all(pieces, "dp", 0, 0),
        lambda pieces: pieces,
        temporal_out.T.reshape(n_dp, piece, rows),
    )
    base = unpack_own(
        halves[0], temporal_out, token_rows, own_shards, temporal_pieces, piece
    )
    base, w_first, w_second = unpack_other(
        halves[1], temporal_out, base, own_shards, crossed, other_shards, piece, held
    )

    code = code_index.astype(jnp.int32).reshape(1)
    sizes = (rows, hidden, width)
    state_type = jax.ShapeDtypeStruct((rows, width), BF16)
    got = []
    for step in range(n_code - 1):
        (state,) = turn(
            functools.partial(forward_kernel, step),
            (code, base, w_first, w_second, *got[-1:]),
            [state_type], "forward_turn", sizes,
        )
        got.append(hop(state, "code", step, step + 1))
    unit, scale, normed, slope, active = turn(
        saved_kernel,
        (base, w_first, *got),
        [
            jax.ShapeDtypeStruct((rows, width), F32),
            jax.ShapeDtypeStruct((rows, 1), F32),
            state_type,
            jax.ShapeDtypeStruct((rows, hidden), F32),
            jax.ShapeDtypeStruct((hidden, rows), BF16),
        ],
        "saved_values", sizes,
    )
    by_part = (HALVES, n_dp // HALVES, held, rows)

    def exchanged(_, temporal, active):
        pieces = in_dp_order(active.reshape(by_part), half)
        return lax.all_to_all(jnp.concatenate([temporal, pieces], axis=1), "dp", 0, 0)

    cotangent = out_grad[:, 0, :].astype(F32) * barge_mask.astype(F32)[:, None]
    got = []
    for owner in range(n_code - 1, 0, -1):
        through = () if got else (normed, active)
        saved = (cotangent, w_first, w_second, unit, scale, slope)
        carried, *passed = turn(
            functools.partial(backward_kernel, owner, len(got[-1:]), len(through)),
            (code, *saved, *got[-1:]),
            [state_type], "backward_turn", sizes, through,
        )
        if passed:
            normed, active = passed
            normed_all = lax.all_gather(normed, "dp", axis=0, tiled=True)
            early = jnp.zeros((n_dp, piece + held, rows), BF16)
            early = lax.cond(
                upper, lambda given, *_: given, exchanged, early, temporal_pieces, active
            )
            w_first, w_second = reload_weights(
                own_shards, other_shards, early, crossing, piece, held
            )
        got.append(hop(carried, "code", owner, owner - 1))
    saved = (cotangent, w_first, w_second, unit, scale, slope)
    late, pre_slope = turn(
        last_kernel, (*saved, *got),
        [
            jax.ShapeDtypeStruct((rows, 2 * width), BF16),
            jax.ShapeDtypeStruct((hidden, rows), BF16),
        ],
        "last_values", sizes,
    )


    def exchanged_active(_, temporal, active):
        pieces = in_dp_order(active.reshape(by_part), half)
        return jnp.concatenate([temporal, lax.all_to_all(pieces, "dp", 0, 0)], axis=1)

    early = lax.cond(
        upper, exchanged_active, lambda given, *_: given, early, temporal_pieces, active
    )
    own_late = gather_half(late, n_dp)
    late_rows, early = lax.optimization_barrier((late, early))
    late_all = (own_late, gather_half(swap_halves(late_rows, n_dp), n_dp))
    temporal_all, active_all = early[:, :piece], early[:, piece:]
    pre_all = lax.all_to_all(in_dp_order(pre_slope.reshape(by_part), half), "dp", 0, 0)
    terms = temporal_terms(
        halves[0], late, own_shards, crossed, other_shards, n_code, piece
    )
    terms, pre_all = lax.optimization_barrier((terms, pre_all))
    terms = lax.all_to_all(terms, "code", 0, 0)
    temporal_grad = jnp.sum(terms.astype(F32), axis=0).astype(BF16)
    first_grad = dot_nn(lanes(pre_all), normed_all).astype(BF16)

    own_vocab = table.shape[0] // n_dp
    vocab_ids = dp_index * own_vocab + lax.broadcasted_iota(jnp.int32, (own_vocab, 1), 0)
    temporal_parts = own_and_other(temporal_all, half)
    token_parts = own_and_other(token_all.reshape(n_dp, rows), half)
    active_parts = own_and_other(active_all, half)
    grads = ()
    for part in range(HALVES):
        onehot = (token_parts[part].reshape(1, -1) == vocab_ids).astype(BF16)
        grads = row_grads(
            (lanes(temporal_parts[part]), onehot, lanes(active_parts[part])),
            late_all[part].reshape(-1, 2 * width),
            grads,
            (piece, own_vocab, own_hidden),
        )
    in_grad, table_grad, second_grad = grads
    return (
        temporal_grad,
        in_grad[None],
        table_grad[None],
        first_grad[:own_hidden].T[None],
        second_grad.T[None],
    )


def solution(mesh):
    in_specs = (
        P("dp", None),
        P("code", "dp", None),
        P("code", None, None),
        P("code", None, "dp"),
        P("code", None, "dp"),
        P(None, "code"),
        P("dp"),
        P("dp", "code", None),
    )
    out_specs = (
        P("dp", "code"),
        P("code", "dp", None),
        P("code", "dp", None),
        P("code", None, "dp"),
        P("code", None, "dp"),
    )
    return jax.shard_map(
        per_device, mesh=mesh, in_specs=in_specs, out_specs=out_specs, check_vma=False
    )
```

```python
import functools

import jax
import jax.numpy as jnp
from jax import lax
from jax.experimental import pallas as pl
from jax.experimental.pallas import tpu as pltpu
from jax.sharding import PartitionSpec as P

EPS = 1e-06
F32 = jnp.float32
BF16 = jnp.bfloat16
SUBLANES = 8


def dot_nn(left, right):
    return lax.dot_general(left, right, (((1,), (0,)), ((), ())), preferred_element_type=F32)


def dot_nt(left, right):
    return lax.dot_general(left, right, (((1,), (1,)), ((), ())), preferred_element_type=F32)


def hop(block, axis, source, target):
    return lax.ppermute(block, axis, [(source, target)])


VMEM = pl.BlockSpec(memory_space=pltpu.VMEM)
ANY = pl.BlockSpec(memory_space=pl.ANY)
SMEM = pl.BlockSpec(memory_space=pltpu.SMEM)
HBM = pl.BlockSpec(memory_space=pltpu.HBM)
HALVES, CORES = 2, 2
CROSSING = 144


def params(megabytes):
    return pltpu.CompilerParams(vmem_limit_bytes=megabytes * 1024 * 1024)


def add_depth(piece, half_ref, t_ref, start, sources, d_ref, d_sem):
    n = sources[0][0].shape[0]
    span = CORES * piece

    def copies(s):
        first = 0
        for i, (ref, count) in enumerate(sources):
            yield pltpu.make_async_copy(
                ref.at[s, pl.ds(0, count)],
                d_ref.at[pl.ds(s * piece + first, count)],
                d_sem.at[i, s],
            )
            first += count

    for s in range(n):
        for copy in copies(s):
            copy.start()

    def total():
        result = start
        for x in range(n // CORES):
            for core in range(CORES):
                for copy in copies(x * CORES + core):
                    copy.wait()
            column = pl.multiple_of((x * HALVES + half_ref[0]) * span, span)
            part = d_ref[pl.ds(x * span, span), :]
            result = result + dot_nn(t_ref[:, pl.ds(column, span)], part)
        return result

    return total


def weight_copies(ref, first, held, part, w1_ref, w2_ref, w_sem):
    n = ref.shape[0]
    return [
        pltpu.make_async_copy(
            ref.at[s, pl.ds(first + which * held, held)],
            to_ref.at[pl.ds((part * n + s) * held, held)],
            w_sem.at[which, s],
        )
        for which, to_ref in enumerate((w1_ref, w2_ref))
        for s in range(n)
    ]


def own_kernel(piece, half_ref, t_ref, start_ref, g_ref, after_ref, base_ref, d_ref, d_sem):
    start = start_ref[...].astype(F32)
    sources = ((g_ref, piece),)
    base_ref[...] = add_depth(piece, half_ref, t_ref, start, sources, d_ref, d_sem)()


def other_kernel(piece, held, crossed, half_ref, t_ref, start_ref, own_ref, r_ref, g_ref,
                 base_ref, w1_ref, w2_ref, d_ref, d_sem, w_sem):
    rest = piece - crossed
    sources = ((r_ref, crossed), (g_ref, rest))
    total = add_depth(piece, half_ref, t_ref, start_ref[...], sources, d_ref, d_sem)
    copies = [
        copy
        for part, (ref, first) in enumerate(((own_ref, piece), (g_ref, rest)))
        for copy in weight_copies(ref, first, held, part, w1_ref, w2_ref, w_sem.at[part])
    ]
    for copy in copies:
        copy.start()
    base_ref[...] = total()
    for copy in copies:
        copy.wait()


def unpack_own(half, temporal, start, own, after, piece):
    rows, width = start.shape
    n = own.shape[0]
    return pl.pallas_call(
        functools.partial(own_kernel, piece),
        in_specs=[SMEM, VMEM, VMEM, HBM, ANY],
        out_specs=VMEM,
        out_shape=jax.ShapeDtypeStruct((rows, width), F32),
        scratch_shapes=[
            pltpu.VMEM((n * piece, width), BF16),
            pltpu.SemaphoreType.DMA((1, n)),
        ],
        compiler_params=params(50),
        name="unpack_own",
    )(half, temporal, start, own, after)


def unpack_other(half, temporal, start, own, crossed, other, piece, held):
    rows, width = start.shape
    n = own.shape[0]
    weight = pltpu.VMEM((HALVES * n * held, width), BF16)
    return pl.pallas_call(
        functools.partial(other_kernel, piece, held, crossed.shape[1]),
        in_specs=[SMEM, VMEM, VMEM, HBM, HBM, HBM],
        out_specs=[VMEM] * 3,
        out_shape=[pltpu.VMEM((rows, width), F32), weight, weight],
        scratch_shapes=[
            pltpu.VMEM((n * piece, width), BF16),
            pltpu.SemaphoreType.DMA((2, n)),
            pltpu.SemaphoreType.DMA((HALVES, 2, n)),
        ],
        compiler_params=params(44),
        name="unpack_other",
    )(half, temporal, start, own, crossed, other)


def reload_kernel(piece, held, crossed, own_ref, g_ref, after_ref, w1_ref, w2_ref, w_sem):
    copies = [
        copy
        for part, (ref, first) in enumerate(((own_ref, piece), (g_ref, piece - crossed)))
        for copy in weight_copies(ref, first, held, part, w1_ref, w2_ref, w_sem.at[part])
    ]
    for copy in copies:
        copy.start()
    for copy in copies:
        copy.wait()


def reload_weights(own, other, after, crossed, piece, held):
    n, _, width = own.shape
    weight = pltpu.VMEM((HALVES * n * held, width), BF16)
    return pl.pallas_call(
        functools.partial(reload_kernel, piece, held, crossed),
        in_specs=[HBM, HBM, ANY],
        out_specs=[VMEM] * 2,
        out_shape=[weight, weight],
        scratch_shapes=[pltpu.SemaphoreType.DMA((HALVES, 2, n))],
        compiler_params=params(44),
        name="reload_weights",
    )(own, other, after)


def normalise(resid):
    scale = lax.rsqrt(jnp.mean(resid * resid, axis=-1, keepdims=True) + EPS)
    return scale, (resid * scale).astype(BF16)


def received(refs, start):
    for ref in refs:
        start = start + ref[...].astype(F32)
    return start


def forward_kernel(turn_index, code_ref, base_ref, w1_ref, w2_ref, *refs):
    out_ref = refs[-1]

    @pl.when(code_ref[0] == turn_index)
    def _():
        resid = received(refs[:-1], base_ref[...])
        _, normed = normalise(resid)
        pre = dot_nt(normed, w1_ref[...])
        active = (pre * jax.nn.sigmoid(pre)).astype(BF16)
        out_ref[...] = (resid + dot_nn(active, w2_ref[...])).astype(BF16)


def saved_kernel(base_ref, w1_ref, *refs):
    unit_ref, scale_ref, normed_ref, slope_ref, active_ref = refs[-5:]
    resid = received(refs[:-5], base_ref[...])
    scale, normed = normalise(resid)
    unit_ref[...] = resid * scale
    scale_ref[...] = scale
    normed_ref[...] = normed
    pre = dot_nt(normed, w1_ref[...])
    sigma = jax.nn.sigmoid(pre)
    slope_ref[...] = sigma * (1.0 + pre * (1.0 - sigma))
    active_ref[...] = (pre * sigma).astype(BF16).T


def backward_math(state_slope, w1_ref, w2_ref, unit_ref, scale_ref, slope_ref, keep_ref):
    slope_b = state_slope.astype(BF16)
    pre_slope = (dot_nt(slope_b, w2_ref[...]) * slope_ref[...]).astype(BF16)
    if keep_ref is not None:
        keep_ref[...] = pre_slope.T
    norm_slope = dot_nn(pre_slope, w1_ref[...])
    unit = unit_ref[...]
    mean = jnp.mean(norm_slope * unit, axis=-1, keepdims=True)
    carried = state_slope + scale_ref[...] * (norm_slope - unit * mean)
    return carried.astype(BF16), slope_b


def backward_kernel(
    owner, n_got, n_through, code_ref, cot_ref, w1_ref, w2_ref, unit_ref, scale_ref, slope_ref,
    *refs
):
    out_ref = refs[n_got + n_through]

    @pl.when(code_ref[0] == owner)
    def _():
        state_slope = received(refs[:n_got], cot_ref[...])
        out_ref[...], _ = backward_math(
            state_slope, w1_ref, w2_ref, unit_ref, scale_ref, slope_ref, None
        )


def last_kernel(cot_ref, w1_ref, w2_ref, unit_ref, scale_ref, slope_ref, *refs):
    late_ref, pre_ref = refs[-2:]
    width = cot_ref.shape[1]
    state_slope = received(refs[:-2], cot_ref[...])
    late_ref[:, :width], late_ref[:, width:] = backward_math(
        state_slope, w1_ref, w2_ref, unit_ref, scale_ref, slope_ref, pre_ref
    )


def turn(kernel, operands, outs, name, sizes, through=()):
    rows, hidden, width = sizes
    scalar = [SMEM] if operands[0].dtype == jnp.int32 else []
    outs = list(outs)
    count = len(operands)
    return pl.pallas_call(
        kernel,
        in_specs=scalar + [VMEM] * (count - len(scalar)) + [ANY] * len(through),
        out_specs=[VMEM] * len(outs) + [ANY] * len(through),
        out_shape=outs + [jax.ShapeDtypeStruct(array.shape, array.dtype) for array in through],
        input_output_aliases={count + i: len(outs) + i for i in range(len(through))},
        compiler_params=params(10),
        cost_estimate=pl.CostEstimate(
            flops=4 * rows * hidden * width, bytes_accessed=4 * hidden * width, transcendentals=0
        ),
        name=name,
    )(*operands, *through)


def term_kernel(half_ref, c_ref, own_ref, crossed_ref, other_ref, out_ref):
    _, piece, width = own_ref.shape
    own = own_ref[...].reshape(CORES * piece, width)
    parts = [ref[core] for core in range(CORES) for ref in (crossed_ref, other_ref)]
    other = jnp.concatenate(parts, axis=0)
    for part, half in ((own, half_ref[0]), (other, 1 - half_ref[0])):
        out_ref[half] = dot_nt(c_ref[...], part).astype(BF16)


def temporal_terms(half, late, own, crossed, other, n_code, piece):
    rows = late.shape[0]
    n, _, width = own.shape
    total = 2 * n * piece
    first = crossed.shape[1]
    weight = lambda count: pl.BlockSpec((CORES, count, width), lambda x: (x, 0, 0))
    return pl.pallas_call(
        term_kernel,
        grid=(n // CORES,),
        in_specs=[
            SMEM,
            pl.BlockSpec((rows, width), lambda x: (0, 0)),
            weight(piece),
            weight(first),
            weight(piece - first),
        ],
        out_specs=pl.BlockSpec((HALVES, rows, total // n_code), lambda x: (x, 0, 0)),
        out_shape=jax.ShapeDtypeStruct((n_code, rows, total // n_code), BF16),
        compiler_params=params(50),
        cost_estimate=pl.CostEstimate(
            flops=2 * rows * width * total, bytes_accessed=2 * width * total, transcendentals=0
        ),
        name="temporal_terms",
    )(half, late, own, crossed, other)


def grads_kernel(blocks, final, *refs):
    n = 3
    count = 2 * n + 1 if final else n + 1
    ins, outs, (first_ref, last_ref, g_ref, *given), (g_sem, in_sem) = (
        refs[:count], refs[count:count + n], refs[count + n:-2], refs[-2:]
    )
    width = outs[0].shape[1]
    block = g_ref.shape[0] // blocks
    rows = [pl.ds(i * block, block) for i in range(blocks)]
    split = ins[0].shape[0]
    targets = [
        first_ref.at[pl.ds(0, split)],
        first_ref.at[pl.ds(split, ins[1].shape[0])],
        last_ref,
        *given,
    ]
    sources = [*ins[:n], *ins[n + 1:]]
    others = [
        pltpu.make_async_copy(source, target, in_sem.at[i])
        for i, (source, target) in enumerate(zip(sources, targets))
    ]
    loads = [
        pltpu.make_async_copy(ins[n].at[part], g_ref.at[part], g_sem.at[i])
        for i, part in enumerate(rows)
    ]
    for copy in others[:n] + loads + others[n:]:
        copy.start()
    for copy in others[:n]:
        copy.wait()
    totals = [None, None]
    for load, part in zip(loads, rows):
        load.wait()
        for i, left_ref in enumerate((first_ref, last_ref)):
            product = dot_nn(left_ref[:, part], g_ref[part, pl.ds(i * width, width)])
            totals[i] = product if totals[i] is None else totals[i] + product
    for copy in others[n:]:
        copy.wait()
    totals = [totals[0][:split], totals[0][split:], totals[1]]
    for i, total in enumerate(totals):
        total = total + given[i][...] if final else total
        outs[i][...] = total[: outs[i].shape[0], :].astype(outs[i].dtype)


def row_grads(lefts, gathered, partial, out_rows):
    frames, both = gathered.shape
    width = both // 2
    final = bool(partial)
    blocks = 2 if frames % 512 == 0 else 1
    outs = [
        jax.ShapeDtypeStruct((rows, width), BF16 if final else F32)
        for rows in (out_rows if final else [left.shape[0] for left in lefts])
    ]
    operands = (*lefts, gathered, *partial)
    first = (lefts[0].shape[0] + lefts[1].shape[0], frames)
    return pl.pallas_call(
        functools.partial(grads_kernel, blocks, final),
        in_specs=[HBM] * len(operands),
        out_specs=[VMEM] * len(outs),
        out_shape=outs,
        scratch_shapes=[
            pltpu.VMEM(first, BF16),
            pltpu.VMEM(lefts[2].shape, BF16),
            pltpu.VMEM(gathered.shape, BF16),
            *[pltpu.VMEM(part.shape, F32) for part in partial],
            pltpu.SemaphoreType.DMA((blocks,)),
            pltpu.SemaphoreType.DMA((len(operands) - 1,)),
        ],
        compiler_params=params(58),
        cost_estimate=pl.CostEstimate(
            flops=2 * sum(left.shape[0] for left in lefts) * width * frames,
            bytes_accessed=2 * frames * both,
            transcendentals=0,
        ),
        name="row_grads",
    )(*operands)


def own_and_other(array, half):
    split = array.reshape((-1, HALVES, CORES) + array.shape[1:])
    pick = lambda which: lax.dynamic_index_in_dim(split, which, 1, keepdims=False)
    return tuple(
        part.reshape((-1,) + array.shape[1:]) for part in (pick(half), pick(1 - half))
    )


def in_dp_order(both, half):
    own, other = (part.reshape((-1, 1, CORES) + part.shape[1:]) for part in both)
    ordered = jnp.where(
        half == 0,
        jnp.concatenate([own, other], axis=1),
        jnp.concatenate([other, own], axis=1),
    )
    return ordered.reshape((-1,) + ordered.shape[3:])


def swap_halves(block, n_dp):
    return lax.ppermute(block, "dp", [(i, i ^ CORES) for i in range(n_dp)])


def gather_half(block, n_dp):
    groups = [
        [i for i in range(n_dp) if i // CORES % HALVES == half] for half in range(HALVES)
    ]
    return lax.all_gather(block, "dp", axis=0, axis_index_groups=groups)


def lanes(pieces):
    return pieces.transpose(1, 0, 2).reshape(pieces.shape[1], -1)


def per_device(
    temporal_out, depth_in, embed, depth_w1, depth_w2, audio_tokens, barge_mask, out_grad
):
    dp_index = lax.axis_index("dp")
    n_dp, n_code = lax.axis_size("dp"), lax.axis_size("code")
    rows = temporal_out.shape[0]
    piece, width = depth_in.shape[1:]
    own_hidden = depth_w1.shape[2]
    table = embed[0]

    pad_hidden = -own_hidden % SUBLANES
    held = own_hidden + pad_hidden
    hidden = held * n_dp
    pad = ((0, pad_hidden), (0, 0))
    shard = jnp.concatenate(
        [depth_in[0], jnp.pad(depth_w1[0].T, pad), jnp.pad(depth_w2[0].T, pad)], axis=0
    )
    half = (dp_index // CORES % HALVES).astype(jnp.int32)
    halves = (half.reshape(1), 1 - half.reshape(1))
    crossing = CROSSING if piece > CROSSING else piece // 2
    own_shards = gather_half(shard, n_dp)
    other_shards = gather_half(swap_halves(shard[crossing:], n_dp), n_dp)
    core = dp_index % CORES
    split = own_shards[:, :crossing].reshape(-1, CORES, crossing, width)
    mine = swap_halves(lax.dynamic_index_in_dim(split, core, 1, keepdims=False), n_dp)
    theirs = lax.ppermute(mine, "dp", [(i, i ^ 1) for i in range(n_dp)])
    crossed = jnp.where(
        core == 0, jnp.stack([mine, theirs], axis=1), jnp.stack([theirs, mine], axis=1)
    ).reshape(-1, crossing, width)

    token_all = audio_tokens[:, 0]
    token_own = lax.dynamic_slice_in_dim(token_all, dp_index * rows, rows, 0)
    token_rows = jnp.take(table, token_own, axis=0)
    code_index = lax.axis_index("code")
    upper = code_index >= n_code // 2
    temporal_pieces = lax.cond(
        upper,
        lambda pieces: lax.all_to_all(pieces, "dp", 0, 0),
        lambda pieces: pieces,
        temporal_out.T.reshape(n_dp, piece, rows),
    )
    base = unpack_own(
        halves[0], temporal_out, token_rows, own_shards, temporal_pieces, piece
    )
    base, w_first, w_second = unpack_other(
        halves[1], temporal_out, base, own_shards, crossed, other_shards, piece, held
    )

    code = code_index.astype(jnp.int32).reshape(1)
    sizes = (rows, hidden, width)
    state_type = jax.ShapeDtypeStruct((rows, width), BF16)
    got = []
    for step in range(n_code - 1):
        (state,) = turn(
            functools.partial(forward_kernel, step),
            (code, base, w_first, w_second, *got[-1:]),
            [state_type], "forward_turn", sizes,
        )
        got.append(hop(state, "code", step, step + 1))
    unit, scale, normed, slope, active = turn(
        saved_kernel,
        (base, w_first, *got),
        [
            jax.ShapeDtypeStruct((rows, width), F32),
            jax.ShapeDtypeStruct((rows, 1), F32),
            state_type,
            jax.ShapeDtypeStruct((rows, hidden), F32),
            jax.ShapeDtypeStruct((hidden, rows), BF16),
        ],
        "saved_values", sizes,
    )
    by_part = (HALVES, n_dp // HALVES, held, rows)

    def exchanged(_, temporal, active):
        pieces = in_dp_order(active.reshape(by_part), half)
        return lax.all_to_all(jnp.concatenate([temporal, pieces], axis=1), "dp", 0, 0)

    cotangent = out_grad[:, 0, :].astype(F32) * barge_mask.astype(F32)[:, None]
    got = []
    for owner in range(n_code - 1, 0, -1):
        through = () if got else (normed, active)
        saved = (cotangent, w_first, w_second, unit, scale, slope)
        carried, *passed = turn(
            functools.partial(backward_kernel, owner, len(got[-1:]), len(through)),
            (code, *saved, *got[-1:]),
            [state_type], "backward_turn", sizes, through,
        )
        if passed:
            normed, active = passed
            normed_all = lax.all_gather(normed, "dp", axis=0, tiled=True)
            early = jnp.zeros((n_dp, piece + held, rows), BF16)
            early = lax.cond(
                upper, lambda given, *_: given, exchanged, early, temporal_pieces, active
            )
            w_first, w_second = reload_weights(
                own_shards, other_shards, early, crossing, piece, held
            )
        got.append(hop(carried, "code", owner, owner - 1))
    saved = (cotangent, w_first, w_second, unit, scale, slope)
    late, pre_slope = turn(
        last_kernel, (*saved, *got),
        [
            jax.ShapeDtypeStruct((rows, 2 * width), BF16),
            jax.ShapeDtypeStruct((hidden, rows), BF16),
        ],
        "last_values", sizes,
    )


    def exchanged_active(_, temporal, active):
        pieces = in_dp_order(active.reshape(by_part), half)
        return jnp.concatenate([temporal, lax.all_to_all(pieces, "dp", 0, 0)], axis=1)

    early = lax.cond(
        upper, exchanged_active, lambda given, *_: given, early, temporal_pieces, active
    )
    own_late = gather_half(late, n_dp)
    late_rows, early = lax.optimization_barrier((late, early))
    late_all = (own_late, gather_half(swap_halves(late_rows, n_dp), n_dp))
    temporal_all, active_all = early[:, :piece], early[:, piece:]
    pre_all = lax.all_to_all(in_dp_order(pre_slope.reshape(by_part), half), "dp", 0, 0)
    terms = temporal_terms(
        halves[0], late, own_shards, crossed, other_shards, n_code, piece
    )
    terms, pre_all = lax.optimization_barrier((terms, pre_all))
    terms = lax.all_to_all(terms, "code", 0, 0)
    temporal_grad = jnp.sum(terms.astype(F32), axis=0).astype(BF16)
    first_grad = dot_nn(lanes(pre_all), normed_all).astype(BF16)

    own_vocab = table.shape[0] // n_dp
    vocab_ids = dp_index * own_vocab + lax.broadcasted_iota(jnp.int32, (own_vocab, 1), 0)
    temporal_parts = own_and_other(temporal_all, half)
    token_parts = own_and_other(token_all.reshape(n_dp, rows), half)
    active_parts = own_and_other(active_all, half)
    grads = ()
    for part in range(HALVES):
        onehot = (token_parts[part].reshape(1, -1) == vocab_ids).astype(BF16)
        grads = row_grads(
            (lanes(temporal_parts[part]), onehot, lanes(active_parts[part])),
            late_all[part].reshape(-1, 2 * width),
            grads,
            (piece, own_vocab, own_hidden),
        )
    in_grad, table_grad, second_grad = grads
    return (
        temporal_grad,
        in_grad[None],
        table_grad[None],
        first_grad[:own_hidden].T[None],
        second_grad.T[None],
    )


def solution(mesh):
    in_specs = (
        P("dp", None),
        P("code", "dp", None),
        P("code", None, None),
        P("code", None, "dp"),
        P("code", None, "dp"),
        P(None, "code"),
        P("dp"),
        P("dp", "code", None),
    )
    out_specs = (
        P("dp", "code"),
        P("code", "dp", None),
        P("code", "dp", None),
        P("code", None, "dp"),
        P("code", None, "dp"),
    )
    return jax.shard_map(
        per_device, mesh=mesh, in_specs=in_specs, out_specs=out_specs, check_vma=False
    )
```

```python
import functools

import jax
import jax.numpy as jnp
from jax import lax
from jax.experimental import pallas as pl
from jax.experimental.pallas import tpu as pltpu
from jax.sharding import PartitionSpec as P

EPS = 1e-06
F32 = jnp.float32
BF16 = jnp.bfloat16
SUBLANES = 8


def dot_nn(left, right):
    return lax.dot_general(left, right, (((1,), (0,)), ((), ())), preferred_element_type=F32)


def dot_nt(left, right):
    return lax.dot_general(left, right, (((1,), (1,)), ((), ())), preferred_element_type=F32)


def hop(block, axis, source, target):
    return lax.ppermute(block, axis, [(source, target)])


VMEM = pl.BlockSpec(memory_space=pltpu.VMEM)
ANY = pl.BlockSpec(memory_space=pl.ANY)
SMEM = pl.BlockSpec(memory_space=pltpu.SMEM)
HBM = pl.BlockSpec(memory_space=pltpu.HBM)
HALVES, CORES = 2, 2
CROSSING = 144


def params(megabytes):
    return pltpu.CompilerParams(vmem_limit_bytes=megabytes * 1024 * 1024)


def add_depth(piece, half_ref, t_ref, start, sources, d_ref, d_sem):
    n = sources[0][0].shape[0]
    span = CORES * piece

    def copies(s):
        first = 0
        for i, (ref, count) in enumerate(sources):
            yield pltpu.make_async_copy(
                ref.at[s, pl.ds(0, count)],
                d_ref.at[pl.ds(s * piece + first, count)],
                d_sem.at[i, s],
            )
            first += count

    for s in range(n):
        for copy in copies(s):
            copy.start()

    def total():
        result = start
        for x in range(n // CORES):
            for core in range(CORES):
                for copy in copies(x * CORES + core):
                    copy.wait()
            column = pl.multiple_of((x * HALVES + half_ref[0]) * span, span)
            part = d_ref[pl.ds(x * span, span), :]
            result = result + dot_nn(t_ref[:, pl.ds(column, span)], part)
        return result

    return total


def weight_copies(ref, first, held, part, w1_ref, w2_ref, w_sem):
    n = ref.shape[0]
    return [
        pltpu.make_async_copy(
            ref.at[s, pl.ds(first + which * held, held)],
            to_ref.at[pl.ds((part * n + s) * held, held)],
            w_sem.at[which, s],
        )
        for which, to_ref in enumerate((w1_ref, w2_ref))
        for s in range(n)
    ]


def own_kernel(piece, half_ref, t_ref, start_ref, g_ref, after_ref, base_ref, d_ref, d_sem):
    start = start_ref[...].astype(F32)
    sources = ((g_ref, piece),)
    base_ref[...] = add_depth(piece, half_ref, t_ref, start, sources, d_ref, d_sem)()


def other_kernel(piece, held, crossed, half_ref, t_ref, start_ref, own_ref, r_ref, g_ref,
                 base_ref, w1_ref, w2_ref, d_ref, d_sem, w_sem):
    rest = piece - crossed
    sources = ((r_ref, crossed), (g_ref, rest))
    total = add_depth(piece, half_ref, t_ref, start_ref[...], sources, d_ref, d_sem)
    copies = [
        copy
        for part, (ref, first) in enumerate(((own_ref, piece), (g_ref, rest)))
        for copy in weight_copies(ref, first, held, part, w1_ref, w2_ref, w_sem.at[part])
    ]
    for copy in copies:
        copy.start()
    base_ref[...] = total()
    for copy in copies:
        copy.wait()


def unpack_own(half, temporal, start, own, after, piece):
    rows, width = start.shape
    n = own.shape[0]
    return pl.pallas_call(
        functools.partial(own_kernel, piece),
        in_specs=[SMEM, VMEM, VMEM, HBM, ANY],
        out_specs=VMEM,
        out_shape=jax.ShapeDtypeStruct((rows, width), F32),
        scratch_shapes=[
            pltpu.VMEM((n * piece, width), BF16),
            pltpu.SemaphoreType.DMA((1, n)),
        ],
        compiler_params=params(50),
        name="unpack_own",
    )(half, temporal, start, own, after)


def unpack_other(half, temporal, start, own, crossed, other, piece, held):
    rows, width = start.shape
    n = own.shape[0]
    weight = pltpu.VMEM((HALVES * n * held, width), BF16)
    return pl.pallas_call(
        functools.partial(other_kernel, piece, held, crossed.shape[1]),
        in_specs=[SMEM, VMEM, VMEM, HBM, HBM, HBM],
        out_specs=[VMEM] * 3,
        out_shape=[pltpu.VMEM((rows, width), F32), weight, weight],
        scratch_shapes=[
            pltpu.VMEM((n * piece, width), BF16),
            pltpu.SemaphoreType.DMA((2, n)),
            pltpu.SemaphoreType.DMA((HALVES, 2, n)),
        ],
        compiler_params=params(44),
        name="unpack_other",
    )(half, temporal, start, own, crossed, other)


def reload_kernel(piece, held, crossed, own_ref, g_ref, after_ref, w1_ref, w2_ref, w_sem):
    copies = [
        copy
        for part, (ref, first) in enumerate(((own_ref, piece), (g_ref, piece - crossed)))
        for copy in weight_copies(ref, first, held, part, w1_ref, w2_ref, w_sem.at[part])
    ]
    for copy in copies:
        copy.start()
    for copy in copies:
        copy.wait()


def reload_weights(own, other, after, crossed, piece, held):
    n, _, width = own.shape
    weight = pltpu.VMEM((HALVES * n * held, width), BF16)
    return pl.pallas_call(
        functools.partial(reload_kernel, piece, held, crossed),
        in_specs=[HBM, HBM, ANY],
        out_specs=[VMEM] * 2,
        out_shape=[weight, weight],
        scratch_shapes=[pltpu.SemaphoreType.DMA((HALVES, 2, n))],
        compiler_params=params(44),
        name="reload_weights",
    )(own, other, after)


def normalise(resid):
    scale = lax.rsqrt(jnp.mean(resid * resid, axis=-1, keepdims=True) + EPS)
    return scale, (resid * scale).astype(BF16)


def received(refs, start):
    for ref in refs:
        start = start + ref[...].astype(F32)
    return start


def forward_kernel(turn_index, code_ref, base_ref, w1_ref, w2_ref, *refs):
    out_ref = refs[-1]

    @pl.when(code_ref[0] == turn_index)
    def _():
        resid = received(refs[:-1], base_ref[...])
        _, normed = normalise(resid)
        pre = dot_nt(normed, w1_ref[...])
        active = (pre * jax.nn.sigmoid(pre)).astype(BF16)
        out_ref[...] = (resid + dot_nn(active, w2_ref[...])).astype(BF16)


def saved_kernel(base_ref, w1_ref, *refs):
    unit_ref, scale_ref, normed_ref, slope_ref, active_ref = refs[-5:]
    resid = received(refs[:-5], base_ref[...])
    scale, normed = normalise(resid)
    unit_ref[...] = resid * scale
    scale_ref[...] = scale
    normed_ref[...] = normed
    pre = dot_nt(normed, w1_ref[...])
    sigma = jax.nn.sigmoid(pre)
    slope_ref[...] = sigma * (1.0 + pre * (1.0 - sigma))
    active_ref[...] = (pre * sigma).astype(BF16).T


def backward_math(state_slope, w1_ref, w2_ref, unit_ref, scale_ref, slope_ref, keep_ref):
    slope_b = state_slope.astype(BF16)
    pre_slope = (dot_nt(slope_b, w2_ref[...]) * slope_ref[...]).astype(BF16)
    if keep_ref is not None:
        keep_ref[...] = pre_slope.T
    norm_slope = dot_nn(pre_slope, w1_ref[...])
    unit = unit_ref[...]
    mean = jnp.mean(norm_slope * unit, axis=-1, keepdims=True)
    carried = state_slope + scale_ref[...] * (norm_slope - unit * mean)
    return carried.astype(BF16), slope_b


def backward_kernel(
    owner, n_got, n_through, code_ref, cot_ref, w1_ref, w2_ref, unit_ref, scale_ref, slope_ref,
    *refs
):
    out_ref = refs[n_got + n_through]

    @pl.when(code_ref[0] == owner)
    def _():
        state_slope = received(refs[:n_got], cot_ref[...])
        out_ref[...], _ = backward_math(
            state_slope, w1_ref, w2_ref, unit_ref, scale_ref, slope_ref, None
        )


def last_kernel(cot_ref, w1_ref, w2_ref, unit_ref, scale_ref, slope_ref, *refs):
    late_ref, pre_ref = refs[-2:]
    width = cot_ref.shape[1]
    state_slope = received(refs[:-2], cot_ref[...])
    late_ref[:, :width], late_ref[:, width:] = backward_math(
        state_slope, w1_ref, w2_ref, unit_ref, scale_ref, slope_ref, pre_ref
    )


def turn(kernel, operands, outs, name, sizes, through=()):
    rows, hidden, width = sizes
    scalar = [SMEM] if operands[0].dtype == jnp.int32 else []
    outs = list(outs)
    count = len(operands)
    return pl.pallas_call(
        kernel,
        in_specs=scalar + [VMEM] * (count - len(scalar)) + [ANY] * len(through),
        out_specs=[VMEM] * len(outs) + [ANY] * len(through),
        out_shape=outs + [jax.ShapeDtypeStruct(array.shape, array.dtype) for array in through],
        input_output_aliases={count + i: len(outs) + i for i in range(len(through))},
        compiler_params=params(10),
        cost_estimate=pl.CostEstimate(
            flops=4 * rows * hidden * width, bytes_accessed=4 * hidden * width, transcendentals=0
        ),
        name=name,
    )(*operands, *through)


def term_kernel(half_ref, c_ref, own_ref, crossed_ref, other_ref, out_ref):
    _, piece, width = own_ref.shape
    own = own_ref[...].reshape(CORES * piece, width)
    parts = [ref[core] for core in range(CORES) for ref in (crossed_ref, other_ref)]
    other = jnp.concatenate(parts, axis=0)
    for part, half in ((own, half_ref[0]), (other, 1 - half_ref[0])):
        out_ref[half] = dot_nt(c_ref[...], part).astype(BF16)


def temporal_terms(half, late, own, crossed, other, n_code, piece):
    rows = late.shape[0]
    n, _, width = own.shape
    total = 2 * n * piece
    first = crossed.shape[1]
    weight = lambda count: pl.BlockSpec((CORES, count, width), lambda x: (x, 0, 0))
    return pl.pallas_call(
        term_kernel,
        grid=(n // CORES,),
        in_specs=[
            SMEM,
            pl.BlockSpec((rows, width), lambda x: (0, 0)),
            weight(piece),
            weight(first),
            weight(piece - first),
        ],
        out_specs=pl.BlockSpec((HALVES, rows, total // n_code), lambda x: (x, 0, 0)),
        out_shape=jax.ShapeDtypeStruct((n_code, rows, total // n_code), BF16),
        compiler_params=params(50),
        cost_estimate=pl.CostEstimate(
            flops=2 * rows * width * total, bytes_accessed=2 * width * total, transcendentals=0
        ),
        name="temporal_terms",
    )(half, late, own, crossed, other)


def grads_kernel(blocks, final, *refs):
    n = 3
    count = 2 * n + 1 if final else n + 1
    ins, outs, (first_ref, last_ref, g_ref, *given), (g_sem, in_sem) = (
        refs[:count], refs[count:count + n], refs[count + n:-2], refs[-2:]
    )
    width = outs[0].shape[1]
    block = g_ref.shape[0] // blocks
    rows = [pl.ds(i * block, block) for i in range(blocks)]
    split = ins[0].shape[0]
    targets = [
        first_ref.at[pl.ds(0, split)],
        first_ref.at[pl.ds(split, ins[1].shape[0])],
        last_ref,
        *given,
    ]
    sources = [*ins[:n], *ins[n + 1:]]
    others = [
        pltpu.make_async_copy(source, target, in_sem.at[i])
        for i, (source, target) in enumerate(zip(sources, targets))
    ]
    loads = [
        pltpu.make_async_copy(ins[n].at[part], g_ref.at[part], g_sem.at[i])
        for i, part in enumerate(rows)
    ]
    for copy in others[:n] + loads + others[n:]:
        copy.start()
    for copy in others[:n]:
        copy.wait()
    totals = [None, None]
    for load, part in zip(loads, rows):
        load.wait()
        for i, left_ref in enumerate((first_ref, last_ref)):
            product = dot_nn(left_ref[:, part], g_ref[part, pl.ds(i * width, width)])
            totals[i] = product if totals[i] is None else totals[i] + product
    for copy in others[n:]:
        copy.wait()
    totals = [totals[0][:split], totals[0][split:], totals[1]]
    for i, total in enumerate(totals):
        total = total + given[i][...] if final else total
        outs[i][...] = total[: outs[i].shape[0], :].astype(outs[i].dtype)


def row_grads(lefts, gathered, partial, out_rows):
    frames, both = gathered.shape
    width = both // 2
    final = bool(partial)
    blocks = 4 if frames % 1024 == 0 else 1
    outs = [
        jax.ShapeDtypeStruct((rows, width), BF16 if final else F32)
        for rows in (out_rows if final else [left.shape[0] for left in lefts])
    ]
    operands = (*lefts, gathered, *partial)
    first = (lefts[0].shape[0] + lefts[1].shape[0], frames)
    return pl.pallas_call(
        functools.partial(grads_kernel, blocks, final),
        in_specs=[HBM] * len(operands),
        out_specs=[VMEM] * len(outs),
        out_shape=outs,
        scratch_shapes=[
            pltpu.VMEM(first, BF16),
            pltpu.VMEM(lefts[2].shape, BF16),
            pltpu.VMEM(gathered.shape, BF16),
            *[pltpu.VMEM(part.shape, F32) for part in partial],
            pltpu.SemaphoreType.DMA((blocks,)),
            pltpu.SemaphoreType.DMA((len(operands) - 1,)),
        ],
        compiler_params=params(58),
        cost_estimate=pl.CostEstimate(
            flops=2 * sum(left.shape[0] for left in lefts) * width * frames,
            bytes_accessed=2 * frames * both,
            transcendentals=0,
        ),
        name="row_grads",
    )(*operands)


def own_and_other(array, half):
    split = array.reshape((-1, HALVES, CORES) + array.shape[1:])
    pick = lambda which: lax.dynamic_index_in_dim(split, which, 1, keepdims=False)
    return tuple(
        part.reshape((-1,) + array.shape[1:]) for part in (pick(half), pick(1 - half))
    )


def in_dp_order(both, half):
    own, other = (part.reshape((-1, 1, CORES) + part.shape[1:]) for part in both)
    ordered = jnp.where(
        half == 0,
        jnp.concatenate([own, other], axis=1),
        jnp.concatenate([other, own], axis=1),
    )
    return ordered.reshape((-1,) + ordered.shape[3:])


def swap_halves(block, n_dp):
    return lax.ppermute(block, "dp", [(i, i ^ CORES) for i in range(n_dp)])


def gather_half(block, n_dp):
    groups = [
        [i for i in range(n_dp) if i // CORES % HALVES == half] for half in range(HALVES)
    ]
    return lax.all_gather(block, "dp", axis=0, axis_index_groups=groups)


def lanes(pieces):
    return pieces.transpose(1, 0, 2).reshape(pieces.shape[1], -1)


def per_device(
    temporal_out, depth_in, embed, depth_w1, depth_w2, audio_tokens, barge_mask, out_grad
):
    dp_index = lax.axis_index("dp")
    n_dp, n_code = lax.axis_size("dp"), lax.axis_size("code")
    rows = temporal_out.shape[0]
    piece, width = depth_in.shape[1:]
    own_hidden = depth_w1.shape[2]
    table = embed[0]

    pad_hidden = -own_hidden % SUBLANES
    held = own_hidden + pad_hidden
    hidden = held * n_dp
    pad = ((0, pad_hidden), (0, 0))
    shard = jnp.concatenate(
        [depth_in[0], jnp.pad(depth_w1[0].T, pad), jnp.pad(depth_w2[0].T, pad)], axis=0
    )
    half = (dp_index // CORES % HALVES).astype(jnp.int32)
    halves = (half.reshape(1), 1 - half.reshape(1))
    crossing = CROSSING if piece > CROSSING else piece // 2
    own_shards = gather_half(shard, n_dp)
    other_shards = gather_half(swap_halves(shard[crossing:], n_dp), n_dp)
    core = dp_index % CORES
    split = own_shards[:, :crossing].reshape(-1, CORES, crossing, width)
    mine = swap_halves(lax.dynamic_index_in_dim(split, core, 1, keepdims=False), n_dp)
    theirs = lax.ppermute(mine, "dp", [(i, i ^ 1) for i in range(n_dp)])
    crossed = jnp.where(
        core == 0, jnp.stack([mine, theirs], axis=1), jnp.stack([theirs, mine], axis=1)
    ).reshape(-1, crossing, width)

    token_all = audio_tokens[:, 0]
    token_own = lax.dynamic_slice_in_dim(token_all, dp_index * rows, rows, 0)
    token_rows = jnp.take(table, token_own, axis=0)
    code_index = lax.axis_index("code")
    upper = code_index >= n_code // 2
    temporal_pieces = lax.cond(
        upper,
        lambda pieces: lax.all_to_all(pieces, "dp", 0, 0),
        lambda pieces: pieces,
        temporal_out.T.reshape(n_dp, piece, rows),
    )
    base = unpack_own(
        halves[0], temporal_out, token_rows, own_shards, temporal_pieces, piece
    )
    base, w_first, w_second = unpack_other(
        halves[1], temporal_out, base, own_shards, crossed, other_shards, piece, held
    )

    code = code_index.astype(jnp.int32).reshape(1)
    sizes = (rows, hidden, width)
    state_type = jax.ShapeDtypeStruct((rows, width), BF16)
    got = []
    for step in range(n_code - 1):
        (state,) = turn(
            functools.partial(forward_kernel, step),
            (code, base, w_first, w_second, *got[-1:]),
            [state_type], "forward_turn", sizes,
        )
        got.append(hop(state, "code", step, step + 1))
    unit, scale, normed, slope, active = turn(
        saved_kernel,
        (base, w_first, *got),
        [
            jax.ShapeDtypeStruct((rows, width), F32),
            jax.ShapeDtypeStruct((rows, 1), F32),
            state_type,
            jax.ShapeDtypeStruct((rows, hidden), F32),
            jax.ShapeDtypeStruct((hidden, rows), BF16),
        ],
        "saved_values", sizes,
    )
    by_part = (HALVES, n_dp // HALVES, held, rows)

    def exchanged(_, temporal, active):
        pieces = in_dp_order(active.reshape(by_part), half)
        return lax.all_to_all(jnp.concatenate([temporal, pieces], axis=1), "dp", 0, 0)

    cotangent = out_grad[:, 0, :].astype(F32) * barge_mask.astype(F32)[:, None]
    got = []
    for owner in range(n_code - 1, 0, -1):
        through = () if got else (normed, active)
        saved = (cotangent, w_first, w_second, unit, scale, slope)
        carried, *passed = turn(
            functools.partial(backward_kernel, owner, len(got[-1:]), len(through)),
            (code, *saved, *got[-1:]),
            [state_type], "backward_turn", sizes, through,
        )
        if passed:
            normed, active = passed
            normed_all = lax.all_gather(normed, "dp", axis=0, tiled=True)
            early = jnp.zeros((n_dp, piece + held, rows), BF16)
            early = lax.cond(
                upper, lambda given, *_: given, exchanged, early, temporal_pieces, active
            )
            w_first, w_second = reload_weights(
                own_shards, other_shards, early, crossing, piece, held
            )
        got.append(hop(carried, "code", owner, owner - 1))
    saved = (cotangent, w_first, w_second, unit, scale, slope)
    late, pre_slope = turn(
        last_kernel, (*saved, *got),
        [
            jax.ShapeDtypeStruct((rows, 2 * width), BF16),
            jax.ShapeDtypeStruct((hidden, rows), BF16),
        ],
        "last_values", sizes,
    )


    def exchanged_active(_, temporal, active):
        pieces = in_dp_order(active.reshape(by_part), half)
        return jnp.concatenate([temporal, lax.all_to_all(pieces, "dp", 0, 0)], axis=1)

    early = lax.cond(
        upper, exchanged_active, lambda given, *_: given, early, temporal_pieces, active
    )
    own_late = gather_half(late, n_dp)
    late_rows, early = lax.optimization_barrier((late, early))
    late_all = (own_late, gather_half(swap_halves(late_rows, n_dp), n_dp))
    temporal_all, active_all = early[:, :piece], early[:, piece:]
    pre_all = lax.all_to_all(in_dp_order(pre_slope.reshape(by_part), half), "dp", 0, 0)
    terms = temporal_terms(
        halves[0], late, own_shards, crossed, other_shards, n_code, piece
    )
    terms, pre_all = lax.optimization_barrier((terms, pre_all))
    terms = lax.all_to_all(terms, "code", 0, 0)
    temporal_grad = jnp.sum(terms.astype(F32), axis=0).astype(BF16)
    first_grad = dot_nn(lanes(pre_all), normed_all).astype(BF16)

    own_vocab = table.shape[0] // n_dp
    vocab_ids = dp_index * own_vocab + lax.broadcasted_iota(jnp.int32, (own_vocab, 1), 0)
    temporal_parts = own_and_other(temporal_all, half)
    token_parts = own_and_other(token_all.reshape(n_dp, rows), half)
    active_parts = own_and_other(active_all, half)
    grads = ()
    for part in range(HALVES):
        onehot = (token_parts[part].reshape(1, -1) == vocab_ids).astype(BF16)
        grads = row_grads(
            (lanes(temporal_parts[part]), onehot, lanes(active_parts[part])),
            late_all[part].reshape(-1, 2 * width),
            grads,
            (piece, own_vocab, own_hidden),
        )
    in_grad, table_grad, second_grad = grads
    return (
        temporal_grad,
        in_grad[None],
        table_grad[None],
        first_grad[:own_hidden].T[None],
        second_grad.T[None],
    )


def solution(mesh):
    in_specs = (
        P("dp", None),
        P("code", "dp", None),
        P("code", None, None),
        P("code", None, "dp"),
        P("code", None, "dp"),
        P(None, "code"),
        P("dp"),
        P("dp", "code", None),
    )
    out_specs = (
        P("dp", "code"),
        P("code", "dp", None),
        P("code", "dp", None),
        P("code", None, "dp"),
        P("code", None, "dp"),
    )
    return jax.shard_map(
        per_device, mesh=mesh, in_specs=in_specs, out_specs=out_specs, check_vma=False
    )
```
